512 devices in a mesh: shot: 16 (over z_hi, y), slab: 32 (over z_lo, x, core).
Axes of the slice: x: 4, y: 4, z: 16 (z_hi: 4, z_lo: 4; z = z_hi * 4 + z_lo), core: 2. Of those that a mesh axis runs over, the one named last changes fastest.
Arguments:
- wave_now: float32 [16, 512, 64, 128], P('shot', 'slab'), may hold values from -6 to 6
- wave_prev: float32 [16, 512, 64, 128], P('shot', 'slab'), may hold values from -6 to 6
- courant: float32 [512, 64, 128], P('slab'), may hold values from 0.05 to 0.2
- forward: bfloat16 [16, 3, 512, 64, 128], P('shot', None, 'slab'), may hold values from -6 to 6
- receivers: int32 [16, 3, 256], P('shot'), may hold values from 0 to 511, as said below
- residual: float32 [16, 3, 256], P('shot'), may hold values from -6 to 6
- aperture: int32 [16, 2], P('shot'), may hold values from 0 to 512, as said below
- latent: bfloat16 [256, 32, 4096], P('slab', 'shot')
- weight: float32 [64, 8], replicated, may hold values from -0.75 to 0.75
Outputs:
- wave_after: float32 [16, 512, 64, 128], P('shot', 'slab')
- wave_before: float32 [16, 512, 64, 128], P('shot', 'slab')
- latent_grad: float32 [256, 32, 4096], P('slab', 'shot')
- weight_grad: float32 [64, 8], replicated
The draws below stay inside these ranges and needn't reach their ends.
Inputs may be any that keep to these rules, and one draw needn't show every extreme that they name: receivers[s,0,r], receivers[s,1,r], receivers[s,2,r] are an x, y and depth cell inside the grid. Each shot's aperture is a range of at least 512 // 4 x cells with aperture[s,0] < aperture[s,1].
All inputs are finite; a program needn't handle non-finite values.
Results may differ from the reference program's by a relative error of at most 0.0003.
Values sent between devices are 32-bit elements; how exact they have to be, the bound alone decides.
No kernel may reach another device: no remote copies, remote signals or barrier semaphores. Data moves between devices by JAX's collectives and lax.ppermute only.
A program may use at most 64 MiB of HBM per device.

```python
import math
import jax
import jax.numpy as jnp
from jax import lax

NY = 64
NZ = 128
STEPS = 3
NREC = 256
CH = 64
SHOTS = 16
NX = 512
LX = 256
LY = 32
LZ = 64


def draw_aperture(key, part):
    key_width, key_start = jax.random.split(key)
    widths = jax.random.randint(key_width, (SHOTS,), NX // 4, NX // 2 + 1)
    starts = jax.random.randint(key_start, (SHOTS,), 0, NX - widths + 1)
    starts = starts.at[0].set(0)
    starts = starts.at[1].set(NX - widths[1])
    return jnp.stack([starts, starts + widths], axis=1).astype(jnp.int32)


def draw_receivers(key, part):
    key_x, key_y, key_z = jax.random.split(key, 3)
    along_x = jax.random.randint(key_x, (SHOTS, NREC), 0, NX)
    along_x = along_x.at[:, 0].set(NX - 1)
    along_x = along_x.at[:, 1].set(0)
    along_y = jax.random.randint(key_y, (SHOTS, NREC), 0, NY)
    along_z = jax.random.randint(key_z, (SHOTS, NREC), 0, min(8, NZ))
    return jnp.stack([along_x, along_y, along_z], axis=1).astype(jnp.int32)


def draw_latent(key, part):
    key_vals, key_rows = jax.random.split(key)
    ramp_x = 1.0 + 2.0 * jnp.arange(LX, dtype=jnp.float32) / max(LX - 1, 1)
    ramp_y = 1.0 + jnp.arange(LY, dtype=jnp.float32) / max(LY - 1, 1)
    ramp = ramp_x[:, None, None] * ramp_y[None, :, None]
    factor = jnp.exp(jax.random.uniform(key_rows, (LX, LY, 1), jnp.float32, -0.69, 0.69))
    values = jnp.clip(jax.random.normal(key_vals, (LX, LY, CH * LZ), jnp.float32), -4.0, 4.0)
    return (values * ramp * factor).astype(jnp.bfloat16)


def block_scale(key, dims, cuts, smallest, high):
    def one(dim, parts):
        draws = jax.random.uniform(jax.random.fold_in(jax.random.fold_in(key, 6), dim), (parts,), jnp.float32, smallest / len(cuts), high / len(cuts))
        return jnp.repeat(jnp.exp(draws), dims[dim] // parts).reshape((-1,) + (1,) * (len(dims) - dim - 1))

    level = one(*cuts[0])
    for cut in cuts[1:]:
        level = level * one(*cut)
    return level


def noise(own_key, extent, spread, bound, pieces=(), kind=jnp.bfloat16):
    result = jax.random.normal(own_key, extent, jnp.float32) * spread
    if len(pieces) > 0:
        result = block_scale(own_key, extent, pieces, -0.22, 0.18) * result
    return jnp.clip(result, min=-bound, max=bound).astype(kind)


def setup_inputs(seed: int = 0) -> dict:
    arg_keys = jax.random.split(jax.random.key(seed), 10)
    wave_now = noise(arg_keys[0], (SHOTS, NX, NY, NZ), 1.0, 6.0, ((0, 16), (1, 32)), jnp.float32)
    wave_prev = noise(arg_keys[1], (SHOTS, NX, NY, NZ), 1.0, 6.0, ((0, 16), (1, 32)), jnp.float32)
    courant = jnp.clip(0.05 + 0.15 * jax.random.uniform(arg_keys[2], (NX, NY, NZ), jnp.float32) ** block_scale(arg_keys[2], (NX, NY, NZ), ((0, 32),), -0.2, 0.2), 0.05, 0.2)
    forward = noise(arg_keys[3], (SHOTS, STEPS, NX, NY, NZ), 1.0, 6.0, ((0, 16), (2, 32)))
    receivers = draw_receivers(jax.random.fold_in(arg_keys[9], 71), 0)
    residual = noise(arg_keys[5], (SHOTS, STEPS, NREC), 1.0, 6.0, ((0, 16),), jnp.float32)
    aperture = draw_aperture(jax.random.fold_in(arg_keys[9], 71), 0)
    latent = draw_latent(jax.random.fold_in(arg_keys[9], 71), 0)
    weight = noise(arg_keys[8], (CH, 8), CH ** -0.5, 0.75, (), jnp.float32)
    return {"wave_now": wave_now, "wave_prev": wave_prev, "courant": courant, "forward": forward, "receivers": receivers, "residual": residual, "aperture": aperture, "latent": latent, "weight": weight}


stencil_weights = (-205.0 / 72.0, 8.0 / 5.0, -1.0 / 5.0, 8.0 / 315.0, -1.0 / 560.0)

def laplace(padded):
    size_x = padded.shape[0] - 8
    size_y = padded.shape[1] - 8
    size_z = padded.shape[2] - 8

    def moved(shift_x, shift_y, shift_z):
        return padded[4 + shift_x:4 + shift_x + size_x, 4 + shift_y:4 + shift_y + size_y, 4 + shift_z:4 + shift_z + size_z]
    total = 3.0 * stencil_weights[0] * moved(0, 0, 0)
    for offset in range(1, 5):
        cycle_sum = moved(offset, 0, 0) + moved(-offset, 0, 0)
        cycle_sum = cycle_sum + moved(0, offset, 0) + moved(0, -offset, 0)
        cycle_sum = cycle_sum + moved(0, 0, offset) + moved(0, 0, -offset)
        total = total + stencil_weights[offset] * cycle_sum
    return total

def reference(wave_now, wave_prev, courant, forward, receivers, residual, aperture, latent, weight):
    afters = []
    befores = []
    velocity_grad = jnp.zeros((NX, NY, NZ), jnp.float32)
    x_cells = jnp.arange(NX, dtype=jnp.int32)[:, None, None]
    for shot_index in range(SHOTS):
        current = wave_now[shot_index]
        previous = wave_prev[shot_index]
        accum = jnp.zeros((NX, NY, NZ), jnp.float32)
        for instant in range(STEPS):
            advanced = 2.0 * current - previous + courant * laplace(jnp.pad(current, 4))
            advanced = advanced.at[receivers[shot_index, 0], receivers[shot_index, 1], receivers[shot_index, 2]].add(residual[shot_index, instant])
            accum = accum + advanced * forward[shot_index, instant].astype(jnp.float32)
            previous = current
            current = advanced
        afters.append(current)
        befores.append(previous)
        inside = (x_cells >= aperture[shot_index, 0]) & (x_cells < aperture[shot_index, 1])
        velocity_grad = velocity_grad + jnp.where(inside, courant * accum, 0.0)
    taps = velocity_grad.reshape(LX, 2, LY, 2, LZ, 2).transpose(0, 2, 4, 1, 3, 5).reshape(LX, LY, LZ, 8)
    latent_grad = jnp.einsum('ijkq,cq->ijck', taps, weight, precision=lax.Precision.HIGHEST).reshape(LX, LY, CH * LZ)
    latent_wide = latent.astype(jnp.float32).reshape(LX, LY, CH, LZ)
    weight_grad = jnp.einsum('ijck,ijkq->cq', latent_wide, taps, precision=lax.Precision.HIGHEST) * (1.0 / math.sqrt(LX * LY * LZ))
    return (jnp.stack(afters), jnp.stack(befores), latent_grad, weight_grad)
```

```python
import math

import jax
import jax.numpy as jnp
from jax import lax
from jax.sharding import Mesh, PartitionSpec as P

STEPS = 3
PARTS = ("zh", "y", "zl", "x", "c")
SHOT = ("zh", "y")
SLAB = ("zl", "x", "c")


stencil_weights = (-205.0 / 72.0, 8.0 / 5.0, -1.0 / 5.0, 8.0 / 315.0, -1.0 / 560.0)


def extended(block, axis, dim, width):
    count = lax.axis_size(axis)
    forward = [(i, i + 1) for i in range(count - 1)]
    backward = [(target, source) for source, target in forward]
    low = lax.ppermute(
        lax.slice_in_dim(block, block.shape[dim] - width, None, axis=dim), axis, forward
    )
    high = lax.ppermute(lax.slice_in_dim(block, 0, width, axis=dim), axis, backward)
    return jnp.concatenate([low, block, high], axis=dim)


def laplace(padded):
    size_x = padded.shape[0] - 8
    size_y = padded.shape[1] - 8
    size_z = padded.shape[2] - 8

    def moved(shift_x, shift_y, shift_z):
        return padded[
            4 + shift_x : 4 + shift_x + size_x,
            4 + shift_y : 4 + shift_y + size_y,
            4 + shift_z : 4 + shift_z + size_z,
        ]

    total = 3.0 * stencil_weights[0] * moved(0, 0, 0)
    for offset in range(1, 5):
        cycle_sum = moved(offset, 0, 0) + moved(-offset, 0, 0)
        cycle_sum = cycle_sum + moved(0, offset, 0) + moved(0, -offset, 0)
        cycle_sum = cycle_sum + moved(0, 0, offset) + moved(0, 0, -offset)
        total = total + stencil_weights[offset] * cycle_sum
    return total


def pad_sides(field):
    return jnp.pad(field, ((0, 0), (4, 4), (4, 4)))


def injections(receivers, residual, first_x, extent, size_y, size_z):
    local_x = receivers[0, 0] - first_x
    valid = (local_x >= 0) & (local_x < extent)
    row = jnp.where(valid, local_x * size_y + receivers[0, 1], -1)
    rows = (row[None, :] == jnp.arange(extent * size_y, dtype=jnp.int32)[:, None]).astype(jnp.float32)
    cols = (receivers[0, 2][:, None] == jnp.arange(size_z, dtype=jnp.int32)[None, :]).astype(jnp.float32)
    spread = residual[0][:, :, None] * cols[None]
    out = jnp.einsum("mr,trz->tmz", rows, spread, precision=lax.Precision.HIGHEST)
    return out.reshape(STEPS, extent, size_y, size_z)


def scatter_sum(chunks, axis):
    return lax.all_to_all(chunks, axis, 0, 0, tiled=True).sum(0)


def share_sum(block, axis):
    count = lax.axis_size(axis)
    wide = jnp.broadcast_to(block[None], (count,) + block.shape)
    return lax.all_to_all(wide, axis, 0, 0, tiled=True).sum(0)


def body(wave_now, wave_prev, courant, forward, receivers, residual, aperture, latent, weight):
    slab_cells = courant.shape[0]
    first_x = lax.axis_index(SLAB) * slab_cells
    current = wave_now[0]
    previous = wave_prev[0]
    added = injections(receivers, residual, first_x, *current.shape)
    accum = jnp.zeros(current.shape, jnp.float32)
    for instant in range(STEPS):
        padded = extended(current, SLAB, 0, 4)
        advanced = 2.0 * current - previous + courant * laplace(pad_sides(padded)) + added[instant]
        accum = accum + advanced * forward[0, instant].astype(jnp.float32)
        previous = current
        current = advanced
    x_cells = first_x + jnp.arange(slab_cells, dtype=jnp.int32)
    inside = (x_cells >= aperture[0, 0]) & (x_cells < aperture[0, 1])
    image = jnp.where(inside[:, None, None], courant * accum, 0.0)
    far, near = lax.axis_size("zh"), lax.axis_size("y")
    tile_rows = image.shape[1] // (far * near)
    rows = image.reshape(slab_cells, far, near, tile_rows, image.shape[2]).transpose(2, 1, 3, 0, 4)
    tile = scatter_sum(scatter_sum(rows, "y"), "zh").transpose(1, 0, 2)
    half_x = slab_cells // 2
    half_y = tile_rows // 2
    half_z = tile.shape[2] // 2
    taps = (
        tile.reshape(half_x, 2, half_y, 2, half_z, 2)
        .transpose(0, 2, 4, 1, 3, 5)
        .reshape(half_x, half_y, half_z, 8)
    )
    channels = weight.shape[0]
    latent_grad = jnp.einsum(
        "ijkq,cq->ijck", taps, weight, precision=lax.Precision.HIGHEST
    ).reshape(half_x, half_y, channels * half_z)
    latent_wide = latent.astype(jnp.float32).reshape(half_x, half_y, channels, half_z)
    partial_grad = jnp.einsum("ijck,ijkq->cq", latent_wide, taps, precision=lax.Precision.HIGHEST)
    latent_cells = (
        latent.shape[0] * lax.axis_size(SLAB) * latent.shape[1] * lax.axis_size(SHOT) * half_z
    )
    total_grad = share_sum(share_sum(partial_grad, ("zh", "zl")), ("y", "x", "c"))
    weight_grad = total_grad * (1.0 / math.sqrt(latent_cells))
    return (current[None], previous[None], latent_grad, weight_grad)


def solution(mesh):
    fine = Mesh(mesh.devices.reshape(4, 4, 4, 4, 2), PARTS)
    return jax.shard_map(
        body,
        mesh=fine,
        in_specs=(
            P(SHOT, SLAB, None, None),
            P(SHOT, SLAB, None, None),
            P(SLAB, None, None),
            P(SHOT, None, SLAB, None, None),
            P(SHOT, None, None),
            P(SHOT, None, None),
            P(SHOT, None),
            P(SLAB, SHOT, None),
            P(),
        ),
        out_specs=(
            P(SHOT, SLAB, None, None),
            P(SHOT, SLAB, None, None),
            P(SLAB, SHOT, None),
            P(),
        ),
        check_vma=False,
    )
```

```python
import math

import jax
import jax.numpy as jnp
import numpy as np
from jax import lax
from jax.experimental import pallas as pl
from jax.experimental.pallas import tpu as pltpu
from jax.sharding import Mesh, PartitionSpec as P

STEPS = 3
PARTS = ("zh", "y", "zl", "x", "c")
SHOT = ("zh", "y")
SLAB = ("zl", "x", "c")
EXT = 16
NY = 64
NZ = 128
F32 = jnp.float32
BF16 = jnp.bfloat16

stencil_weights = (-205.0 / 72.0, 8.0 / 5.0, -1.0 / 5.0, 8.0 / 315.0, -1.0 / 560.0)


def high_low(values):
    high = values.astype(BF16)
    return high, (values - high.astype(np.float32)).astype(BF16)


def band(size, center):
    out = np.zeros((size, size), np.float32)
    for k in range(5):
        for i in range(size - k):
            value = center if k == 0 else stencil_weights[k]
            out[i, i + k] = value
            out[i + k, i] = value
    return out


def constants():
    zh, zl = high_low(band(NZ, 3.0 * stencil_weights[0]))
    yh, yl = high_low(band(NY, 0.0))
    along_z = np.concatenate([zh, zh, zl], axis=0)
    along_y = np.concatenate([yh, yh, yl], axis=1)
    spread = np.zeros((NZ, 2, 2, 2, NZ // 2), np.float32)
    for k in range(NZ // 2):
        for c in range(2):
            for h in range(2):
                spread[2 * k + c, h, c, h, k] = 1.0
    spread = spread.reshape(NZ, 4 * NZ).astype(BF16)
    place = np.zeros((2, 64, 128), np.float32)
    for h in range(2):
        for j in range(2):
            for t in range(32):
                place[h, 32 * j + t, 2 * t + h] = 1.0
    pick = np.zeros((8, 32), np.float32)
    for row in range(32):
        c, a, b = (row >> 3) & 1, (row >> 2) & 1, row & 1
        pick[4 * a + 2 * b + c, row] = 1.0
    return along_z, along_y, spread, place, pick


ALONG_Z, ALONG_Y, SPREAD, PLACE, PICK = constants()


def flat_laplace(u, along_z, along_y):
    high = u.astype(BF16)
    low = (u - high.astype(F32)).astype(BF16)
    rows_h, rows_l = high.reshape(2 * NY, NZ), low.reshape(2 * NY, NZ)
    z_part = jnp.dot(
        jnp.concatenate([rows_h, rows_l, rows_h], axis=1), along_z, preferred_element_type=F32
    )
    wide_h = jnp.concatenate([high[0], high[1]], axis=1)
    wide_l = jnp.concatenate([low[0], low[1]], axis=1)
    y_part = jnp.dot(
        along_y, jnp.concatenate([wide_h, wide_l, wide_h], axis=0), preferred_element_type=F32
    )
    z_part = z_part.reshape(2, NY, NZ)
    return z_part[0] + y_part[:, :NZ], z_part[1] + y_part[:, NZ:]


def across(ref, at):
    total = stencil_weights[1] * (ref[at + 1] + ref[at - 1])
    for k in range(2, 5):
        total = total + stencil_weights[k] * (ref[at + k] + ref[at - k])
    return total


def three_parts(v):
    high = v.astype(BF16)
    rest = v - high.astype(F32)
    mid = rest.astype(BF16)
    low = (rest - mid.astype(F32)).astype(BF16)
    return high, mid, low


def injected(rec, res, first_x, start, planes, steps):
    local = rec[0:1] - first_x - start
    valid = (local >= 0) & (local < planes)
    row = jnp.where(valid, local * NY + rec[1:2], -1)
    count = rec.shape[1]
    cells = lax.broadcasted_iota(jnp.int32, (planes * NY, count), 0)
    rows = jnp.where(cells == row, 1.0, 0.0).astype(BF16)
    depth = lax.broadcasted_iota(jnp.int32, (NZ, count), 0)
    at_depth = depth == rec[2:3]
    out = []
    for t in steps:
        value = jnp.where(at_depth, res[t : t + 1], 0.0)
        total = None
        for part in three_parts(value):
            piece = lax.dot_general(
                rows, part, (((1,), (1,)), ((), ())), preferred_element_type=F32
            )
            total = piece if total is None else total + piece
        out.append(total)
    return out


def head_kernel(
    place, cur, prev, cour, rec, res, along_z, along_y, up_msg, down_msg, middle
):
    tz, ty = along_z[...], along_y[...]
    (added,) = injected(rec[...], res[...], place[0], 4, 8, (0,))
    added = added.reshape(8, NY, NZ)
    for pair in range(4):
        at = 4 + 2 * pair
        flat = flat_laplace(cur[at : at + 2], tz, ty)
        for e in range(2):
            lap = flat[e] + across(cur, at + e)
            value = 2.0 * cur[at + e] - prev[at + e] + cour[at + e] * lap
            middle[2 * pair + e] = value + added[2 * pair + e]
    up_msg[0:4] = middle[4:8]
    up_msg[4:12] = cur[8:16]
    up_msg[12:16] = prev[12:16]
    up_msg[16:20] = cour[12:16]
    down_msg[0:4] = middle[0:4]
    down_msg[4:12] = cur[0:8]
    down_msg[12:16] = prev[0:4]
    down_msg[16:20] = cour[0:4]


def inject_kernel(place, rec, res, out):
    fields = injected(rec[...], res[...], place[0], -4, EXT + 8, range(STEPS))
    for t in range(STEPS):
        out[t] = fields[t].reshape(EXT + 8, NY, NZ)


def wave_kernel(
    place, cur, prev, cour, fwd, middle, added, low_msg, high_msg, along_z, along_y,
    rows, after, before, c0, c1, c2, co, pv,
):
    c0[0:8] = low_msg[4:12]
    c0[8:24] = cur[...]
    c0[24:32] = high_msg[4:12]
    co[0:4] = low_msg[16:20]
    co[4:20] = cour[...]
    co[20:24] = high_msg[16:20]
    pv[0:4] = low_msg[12:16]
    pv[4:20] = prev[...]
    pv[20:24] = high_msg[12:16]
    c1[0:4] = low_msg[0:4]
    c1[12:20] = middle[...]
    c1[28:32] = high_msg[0:4]
    tz, ty = along_z[...], along_y[...]
    for x in (-4, -2, 0, 2, 12, 14, 16, 18):
        flat = flat_laplace(c0[x + 8 : x + 10], tz, ty)
        for e in range(2):
            i = x + e
            lap = flat[e] + across(c0, i + 8)
            value = 2.0 * c0[i + 8] - pv[i + 4] + co[i + 4] * lap
            c1[i + 8] = value + added[0, i + 4]
    for x in range(-4, EXT + 4, 2):
        flat = flat_laplace(c1[x + 8 : x + 10], tz, ty)
        for e in range(2):
            i = x + e
            lap = flat[e] + across(c1, i + 8)
            value = 2.0 * c1[i + 8] - c0[i + 8] + co[i + 4] * lap + added[1, i + 4]
            c2[i + 4] = value
            if 0 <= i < EXT:
                before[i] = value
    lower = lax.broadcasted_iota(jnp.int32, (NY, NZ), 0) % 8 < 4
    for x in range(0, EXT, 2):
        flat = flat_laplace(c2[x + 4 : x + 6], tz, ty)
        images = []
        for e in range(2):
            i = x + e
            lap = flat[e] + across(c2, i + 4)
            value = 2.0 * c2[i + 4] - c1[i + 8] + co[i + 4] * lap + added[2, i + 4]
            after[i] = value
            acc = c1[i + 8] * fwd[0, i].astype(F32)
            acc = acc + c2[i + 4] * fwd[1, i].astype(F32)
            acc = acc + value * fwd[2, i].astype(F32)
            at = place[0] + i
            inside = (at >= place[1]) & (at < place[2])
            images.append(jnp.where(inside, co[i + 4] * acc, 0.0))
        first, second = images
        even = jnp.where(lower, first, pltpu.roll(second, 4, 0)).reshape(4, 2, 8, NZ)
        odd = jnp.where(lower, pltpu.roll(first, NY - 4, 0), second).reshape(4, 2, 8, NZ)
        for far in range(4):
            for half in range(2):
                rows[2 * half, far, x // 2] = even[far, half]
                rows[2 * half + 1, far, x // 2] = odd[far, half]


def decode_kernel(pieces, spread, latent, place, pick, taps, shares):
    tile = ((pieces[0] + pieces[1]) + (pieces[2] + pieces[3])).reshape(64, NZ)
    wide = None
    for part in three_parts(tile):
        piece = jnp.dot(part, spread[...], preferred_element_type=F32)
        wide = piece if wide is None else wide + piece
    for i in range(8):
        for block in range(4):
            taps[8 * block : 8 * block + 8, NZ * i : NZ * (i + 1)] = wide[
                8 * i : 8 * i + 8, NZ * block : NZ * (block + 1)
            ]
    grad = None
    for part in three_parts(taps[...]):
        piece = lax.dot_general(
            part, latent[...], (((1,), (1,)), ((), ())), preferred_element_type=F32
        )
        grad = piece if grad is None else grad + piece
    tap_j = (lax.broadcasted_iota(jnp.int32, (32, 64), 0) >> 1) & 1
    lane_j = lax.broadcasted_iota(jnp.int32, (32, 64), 1) >> 5
    grad = jnp.where(tap_j == lane_j, grad, 0.0)
    exact = dict(preferred_element_type=F32, precision=lax.Precision.HIGHEST)
    moved = jnp.concatenate(
        [jnp.dot(grad[:16], place[0], **exact), jnp.dot(grad[16:], place[1], **exact)], axis=0
    )
    total = jnp.dot(pick[...], moved, **exact)
    shares[...] = jnp.broadcast_to(total[None], shares.shape)


def latent_kernel(mix, taps, out):
    wide = jnp.dot(
        mix[...], taps[...], preferred_element_type=F32, precision=lax.Precision.HIGHEST
    )
    for i in range(8):
        out[64 * i : 64 * (i + 1)] = wide[:, NZ * i : NZ * (i + 1)]


def share_kernel(pieces, shares):
    total = jnp.sum(pieces[...], axis=0, keepdims=True)
    shares[...] = jnp.broadcast_to(total, shares.shape)


def final_kernel(pieces, out, *, scale):
    out[...] = jnp.sum(pieces[...], axis=0)[:, :64] * scale


VM = pl.BlockSpec(memory_space=pltpu.VMEM)
SM = pl.BlockSpec(memory_space=pltpu.SMEM)


def call(kernel, name, args, outs, scratch=(), scalars=0, interpret=False):
    return pl.pallas_call(
        kernel,
        name=name,
        in_specs=[SM] * scalars + [VM] * (len(args) - scalars),
        out_specs=[VM] * len(outs),
        out_shape=[jax.ShapeDtypeStruct(*o) for o in outs],
        scratch_shapes=list(scratch),
        compiler_params=pltpu.CompilerParams(vmem_limit_bytes=48 << 20),
        interpret=interpret,
    )(*args)


def head(place, cur, prev, cour, rec, res, **kw):
    plane = (NY, NZ)
    return call(
        head_kernel, "head", (place, cur, prev, cour, rec, res, ALONG_Z, ALONG_Y),
        [((20,) + plane, F32), ((20,) + plane, F32), ((8,) + plane, F32)], scalars=1, **kw,
    )


def inject(place, rec, res, **kw):
    outs = [((STEPS, EXT + 8, NY, NZ), F32)]
    return call(inject_kernel, "inject", (place, rec, res), outs, scalars=1, **kw)[0]


def wave(place, cur, prev, cour, fwd, middle, added, low_msg, high_msg, **kw):
    plane = (NY, NZ)
    return call(
        wave_kernel, "wave",
        (place, cur, prev, cour, fwd, middle, added, low_msg, high_msg, ALONG_Z, ALONG_Y),
        [((4, 4, 8, 8, NZ), F32), ((EXT,) + plane, F32), ((EXT,) + plane, F32)],
        [pltpu.VMEM((n,) + plane, F32) for n in (32, 32, 24, 24, 24)], scalars=1, **kw,
    )


def decode(pieces, latent, **kw):
    return call(
        decode_kernel, "decode", (pieces, SPREAD, latent, PLACE, PICK),
        [((32, 8 * NZ), F32), ((16, 8, 128), F32)], **kw,
    )


def latent_rows(latent):
    return latent.reshape(8, 2, 32, NZ).transpose(1, 2, 0, 3).reshape(64, 8 * NZ)


def mixing(weight):
    taps = weight.reshape(32, 2, 2, 2, 2).transpose(0, 1, 4, 2, 3)
    same = np.eye(2, dtype=np.float32)[None, :, None, None, None, :, None]
    return (taps[:, None, :, :, :, None, :] * same).reshape(64, 32)


def latent_out(mix, taps, **kw):
    flat = call(latent_kernel, "latent", (mix, taps), [((512, NZ), F32)], **kw)[0]
    return flat.reshape(8, 32, 2, NZ).transpose(0, 2, 1, 3).reshape(8, 2, 4096)


def body(wave_now, wave_prev, courant, forward, receivers, residual, aperture, latent, weight):
    first_x = lax.axis_index(SLAB) * EXT
    place = jnp.concatenate([first_x[None].astype(jnp.int32), aperture[0]])
    cur, prev = wave_now[0], wave_prev[0]
    rec, res = receivers[0], residual[0]
    up_msg, down_msg, middle = head(place, cur, prev, courant, rec, res)
    count = lax.axis_size(SLAB)
    pairs = [(i, i + 1) for i in range(count - 1)]
    low_msg = lax.ppermute(up_msg, SLAB, pairs)
    high_msg = lax.ppermute(down_msg, SLAB, [(b, a) for a, b in pairs])
    added = inject(place, rec, res)
    lat = latent_rows(latent)
    mix = mixing(weight)
    rows, after, before = wave(
        place, cur, prev, courant, forward[0], middle, added, low_msg, high_msg
    )
    near = lax.all_to_all(rows, "y", 0, 0, tiled=True).sum(0)
    pieces = lax.all_to_all(near, "zh", 0, 0, tiled=True)
    taps, shares = decode(pieces, lat)
    shares = lax.all_to_all(shares, ("zh", "zl"), 0, 0, tiled=True)
    shares = call(share_kernel, "share", (shares,), [((32, 8, 128), F32)])[0]
    shares = lax.all_to_all(shares, ("y", "x", "c"), 0, 0, tiled=True)
    latent_grad = latent_out(mix, taps)

    def last(pieces, out):
        final_kernel(pieces, out, scale=1.0 / math.sqrt(256 * 32 * 64))

    weight_grad = call(last, "total", (shares,), [((8, 64), F32)])[0].T
    return (after[None], before[None], latent_grad, weight_grad)


def solution(mesh):
    fine = Mesh(mesh.devices.reshape(4, 4, 4, 4, 2), PARTS)
    return jax.shard_map(
        body,
        mesh=fine,
        in_specs=(
            P(SHOT, SLAB, None, None),
            P(SHOT, SLAB, None, None),
            P(SLAB, None, None),
            P(SHOT, None, SLAB, None, None),
            P(SHOT, None, None),
            P(SHOT, None, None),
            P(SHOT, None),
            P(SLAB, SHOT, None),
            P(),
        ),
        out_specs=(
            P(SHOT, SLAB, None, None),
            P(SHOT, SLAB, None, None),
            P(SLAB, SHOT, None),
            P(),
        ),
        check_vma=False,
    )
```

```python
import math

import jax
import jax.numpy as jnp
import numpy as np
from jax import lax
from jax.experimental import pallas as pl
from jax.experimental.pallas import tpu as pltpu
from jax.sharding import Mesh, PartitionSpec as P

STEPS = 3
PARTS = ("zh", "y", "zl", "x", "c")
SHOT = ("zh", "y")
SLAB = ("zl", "x", "c")
EXT = 16
NY = 64
NZ = 128
F32 = jnp.float32
BF16 = jnp.bfloat16

stencil_weights = (-205.0 / 72.0, 8.0 / 5.0, -1.0 / 5.0, 8.0 / 315.0, -1.0 / 560.0)


def high_low(values):
    high = values.astype(BF16)
    return high, (values - high.astype(np.float32)).astype(BF16)


def band(size, center):
    out = np.zeros((size, size), np.float32)
    for k in range(5):
        for i in range(size - k):
            value = center if k == 0 else stencil_weights[k]
            out[i, i + k] = value
            out[i + k, i] = value
    return out


def constants():
    zh, zl = high_low(band(NZ, 3.0 * stencil_weights[0]))
    yh, yl = high_low(band(NY, 0.0))
    along_z = np.concatenate([zh, zh, zl], axis=0)
    along_y = np.concatenate([yh, yh, yl], axis=1)
    spread = np.zeros((NZ, 2, 2, 2, NZ // 2), np.float32)
    for k in range(NZ // 2):
        for c in range(2):
            for h in range(2):
                spread[2 * k + c, h, c, h, k] = 1.0
    spread = spread.reshape(NZ, 4 * NZ).astype(BF16)
    place = np.zeros((2, 64, 128), np.float32)
    for h in range(2):
        for j in range(2):
            for t in range(32):
                place[h, 32 * j + t, 2 * t + h] = 1.0
                place[h, 32 * j + t, 64 + 2 * t + h] = 1.0
    pick = np.zeros((8, 32), np.float32)
    for row in range(32):
        c, a, b = (row >> 3) & 1, (row >> 2) & 1, row & 1
        pick[4 * a + 2 * b + c, row] = 1.0
    return along_z, along_y, spread, place, pick


ALONG_Z, ALONG_Y, SPREAD, PLACE, PICK = constants()


def flat_laplace(planes, along_z, along_y):
    count = len(planes)
    high = [u.astype(BF16) for u in planes]
    low = [(u - h.astype(F32)).astype(BF16) for u, h in zip(planes, high)]
    rows_h, rows_l = jnp.concatenate(high, axis=0), jnp.concatenate(low, axis=0)
    z_part = jnp.dot(
        jnp.concatenate([rows_h, rows_l, rows_h], axis=1), along_z, preferred_element_type=F32
    )
    wide_h, wide_l = jnp.concatenate(high, axis=1), jnp.concatenate(low, axis=1)
    y_part = jnp.dot(
        along_y, jnp.concatenate([wide_h, wide_l, wide_h], axis=0), preferred_element_type=F32
    )
    return [z_part[NY * e : NY * (e + 1)] + y_part[:, NZ * e : NZ * (e + 1)] for e in range(count)]


def across(get, at):
    total = stencil_weights[1] * (get(at + 1) + get(at - 1))
    for k in range(2, 5):
        total = total + stencil_weights[k] * (get(at + k) + get(at - k))
    return total


def three_parts(v):
    high = v.astype(BF16)
    rest = v - high.astype(F32)
    mid = rest.astype(BF16)
    low = (rest - mid.astype(F32)).astype(BF16)
    return high, mid, low


def injected(rec, res, first_x, start, planes, steps):
    local = rec[0] - first_x - start
    valid = (local >= 0) & (local < planes)
    row = jnp.where(valid, local * NY + rec[1], -1)
    count = rec.shape[2]
    cells = lax.broadcasted_iota(jnp.int32, (planes * NY, count), 0)
    rows = jnp.where(cells == row, 1.0, 0.0).astype(BF16)
    depth = lax.broadcasted_iota(jnp.int32, (NZ, count), 0)
    at_depth = depth == rec[2]
    out = []
    for t in steps:
        value = jnp.where(at_depth, res[t], 0.0)
        total = None
        for part in three_parts(value):
            piece = lax.dot_general(
                rows, part, (((1,), (1,)), ((), ())), preferred_element_type=F32
            )
            total = piece if total is None else total + piece
        out.append(total)
    return out


def head_kernel(
    first_x, cur_in, prev_in, cour_in, rec_in, res_in, z_in, y_in, outer, inner, begun,
    cur, prev, cour, rec, res, along_z, along_y, sems,
):
    copies = [
        pltpu.make_async_copy(source, target, sems.at[k])
        for k, (source, target) in enumerate(
            (
                (rec_in, rec),
                (res_in, res),
                (cur_in, cur.at[4:20]),
                (z_in, along_z),
                (y_in, along_y),
                (prev_in, prev),
                (cour_in, cour),
            )
        )
    ]
    for copy in copies:
        copy.start()
    zero = jnp.zeros((4, NY, NZ), F32)
    cur[0:4] = zero
    cur[20:24] = zero
    copies[0].wait()
    copies[1].wait()
    (added,) = injected(rec[...], res[...], first_x[0], 0, EXT, (0,))
    for copy in copies[2:]:
        copy.wait()
    tz, ty = along_z[...], along_y[...]
    for group in range(0, EXT, 4):
        flat = flat_laplace([cur[group + e + 4] for e in range(4)], tz, ty)
        for e in range(4):
            i = group + e
            lap = flat[e] + across(lambda at: cur[at + 4], i)
            value = 2.0 * cur[i + 4] - prev[i] + cour[i] * lap
            begun[i] = value + added[NY * i : NY * (i + 1)]
    odd = (first_x[0] >> 4) & 1
    for message, side in ((outer, odd), (inner, 1 - odd)):
        message[0:8] = begun[pl.ds(8 * side, 8)]
        message[8:12] = cur[pl.ds(4 + 12 * side, 4)]
        message[12:16] = cour[pl.ds(12 * side, 4)]


def inject_kernel(first_x, rec, res, second, third):
    one, two = injected(rec[...], res[...], first_x[0], -4, EXT + 8, (1, 2))
    second[...] = one.reshape(EXT + 8, NY, NZ)
    third[...] = two.reshape(EXT + 8, NY, NZ)[4:20]


def wave_kernel(
    first_x, aperture, cur, cour, fwd_in, begun, second, third, outer, inner, along_z, along_y,
    rows, after, before, far_u, far_c, far_k, near_u, mid, fwd, sem,
):
    copy = pltpu.make_async_copy(fwd_in, fwd, sem)
    copy.start()
    odd = (first_x[0] >> 4) & 1
    for message, side in ((outer, odd), (inner, 1 - odd)):
        far_u[pl.ds(8 * side, 8)] = message[0:8]
        far_c[pl.ds(4 * side, 4)] = message[8:12]
        far_k[pl.ds(4 * side, 4)] = message[12:16]

    def courant_at(i):
        return far_k[i + 4] if i < 0 else far_k[i - 12] if i >= EXT else cour[i]

    def now_at(i):
        return far_c[i + 4] if i < 0 else far_c[i - 12] if i >= EXT else cur[i]

    def step_at(i):
        if i < 0:
            return far_u[i + 8]
        if i >= EXT:
            return far_u[i - 8]
        if i < 4:
            return near_u[i]
        return near_u[i - 8] if i >= 12 else begun[i]

    def missing(i, others):
        total = None
        for k in range(1, 5):
            for at in (i - k, i + k):
                if at in others:
                    term = stencil_weights[k] * now_at(at)
                    total = term if total is None else total + term
        return courant_at(i) * total

    for i in range(4):
        near_u[i] = begun[i] + missing(i, range(-4, 0))
        near_u[i + 4] = begun[i + 12] + missing(i + 12, range(16, 20))
        far_u[i + 4] = far_u[i + 4] + missing(i - 4, range(0, 4))
        far_u[i + 8] = far_u[i + 8] + missing(i + 16, range(12, 16))
    tz, ty = along_z[...], along_y[...]
    for group in range(-4, EXT + 4, 4):
        flat = flat_laplace([step_at(group + e) for e in range(4)], tz, ty)
        for e in range(4):
            i = group + e
            lap = flat[e] + across(step_at, i)
            value = 2.0 * step_at(i) - now_at(i) + courant_at(i) * lap + second[i + 4]
            mid[i + 4] = value
            if 0 <= i < EXT:
                before[i] = value
    copy.wait()
    lower = lax.broadcasted_iota(jnp.int32, (NY, NZ), 0) % 8 < 4
    for group in range(0, EXT, 4):
        flat = flat_laplace([mid[group + e + 4] for e in range(4)], tz, ty)
        images = []
        for e in range(4):
            i = group + e
            lap = flat[e] + across(lambda at: mid[at + 4], i)
            value = 2.0 * mid[i + 4] - step_at(i) + cour[i] * lap + third[i]
            after[i] = value
            acc = step_at(i) * fwd[0, i].astype(F32)
            acc = acc + mid[i + 4] * fwd[1, i].astype(F32)
            acc = acc + value * fwd[2, i].astype(F32)
            at = first_x[0] + i
            inside = (at >= aperture[0, 0]) & (at < aperture[0, 1])
            images.append(jnp.where(inside, cour[i] * acc, 0.0))
        for p in range(2):
            first, next_one = images[2 * p : 2 * p + 2]
            even = jnp.where(lower, first, pltpu.roll(next_one, 4, 0)).reshape(4, 2, 8, NZ)
            odds = jnp.where(lower, pltpu.roll(first, NY - 4, 0), next_one).reshape(4, 2, 8, NZ)
            for far in range(4):
                for half in range(2):
                    rows[2 * half, far, group // 2 + p] = even[far, half]
                    rows[2 * half + 1, far, group // 2 + p] = odds[far, half]


def decode_kernel(pieces, spread, latent, place, pick, taps, shares):
    tile = ((pieces[0] + pieces[1]) + (pieces[2] + pieces[3])).reshape(64, NZ)
    wide = None
    for part in three_parts(tile):
        piece = jnp.dot(part, spread[...], preferred_element_type=F32)
        wide = piece if wide is None else wide + piece
    for i in range(8):
        for block in range(4):
            taps[8 * block : 8 * block + 8, NZ * i : NZ * (i + 1)] = wide[
                8 * i : 8 * i + 8, NZ * block : NZ * (block + 1)
            ]
    grad = None
    for part in three_parts(taps[...]):
        piece = lax.dot_general(
            part, latent[...], (((1,), (1,)), ((), ())), preferred_element_type=F32
        )
        grad = piece if grad is None else grad + piece
    tap_j = (lax.broadcasted_iota(jnp.int32, (32, 64), 0) >> 1) & 1
    lane_j = lax.broadcasted_iota(jnp.int32, (32, 64), 1) >> 5
    grad = jnp.where(tap_j == lane_j, grad, 0.0)
    exact = dict(preferred_element_type=F32, precision=lax.Precision.HIGHEST)
    moved = jnp.concatenate(
        [jnp.dot(grad[:16], place[0], **exact), jnp.dot(grad[16:], place[1], **exact)], axis=0
    )
    total = jnp.dot(pick[...], moved, **exact)
    left = lax.broadcasted_iota(jnp.int32, (4, 128), 1) < 64
    packed = jnp.where(left, total[0:4], total[4:8])
    shares[...] = jnp.broadcast_to(packed[None], shares.shape)


def latent_kernel(mix, taps, out):
    wide = jnp.dot(
        mix[...], taps[...], preferred_element_type=F32, precision=lax.Precision.HIGHEST
    )
    for i in range(8):
        out[64 * i : 64 * (i + 1)] = wide[:, NZ * i : NZ * (i + 1)]


def share_kernel(pieces, shares):
    total = jnp.sum(pieces[...], axis=0, keepdims=True)
    shares[...] = jnp.broadcast_to(total, shares.shape)


def final_kernel(pieces, out, *, scale):
    total = jnp.sum(pieces[...], axis=0) * scale
    out[0:4] = total[:, :64]
    out[4:8] = total[:, 64:]


VM = pl.BlockSpec(memory_space=pltpu.VMEM)
SM = pl.BlockSpec(memory_space=pltpu.SMEM)


HB = pl.BlockSpec(memory_space=pltpu.HBM)


def call(kernel, name, args, outs, scratch=(), scalars=0, stay=(), interpret=False):
    specs = [SM] * scalars + [VM] * (len(args) - scalars)
    args = list(args)
    for k in stay:
        specs[k] = HB
        if not interpret:
            args[k] = pltpu.with_memory_space_constraint(jnp.asarray(args[k]), pltpu.HBM)
    return pl.pallas_call(
        kernel,
        name=name,
        in_specs=specs,
        out_specs=[VM] * len(outs),
        out_shape=[jax.ShapeDtypeStruct(*o) for o in outs],
        scratch_shapes=list(scratch),
        compiler_params=pltpu.CompilerParams(vmem_limit_bytes=16 << 20),
        interpret=interpret,
    )(*args)


def planes(count):
    return (count, NY, NZ)


def head(first_x, cur, prev, cour, rec, res, **kw):
    return call(
        head_kernel, "head", (first_x, cur, prev, cour, rec, res, ALONG_Z, ALONG_Y),
        [(planes(EXT), F32)] * 3,
        [
            pltpu.VMEM(planes(EXT + 8), F32), pltpu.VMEM(planes(EXT), F32),
            pltpu.VMEM(planes(EXT), F32), pltpu.VMEM(rec.shape, jnp.int32),
            pltpu.VMEM(res.shape, F32), pltpu.VMEM(ALONG_Z.shape, BF16),
            pltpu.VMEM(ALONG_Y.shape, BF16), pltpu.SemaphoreType.DMA((7,)),
        ],
        scalars=1, stay=range(1, 8), **kw,
    )


def inject(first_x, rec, res, **kw):
    outs = [(planes(EXT + 8), F32), (planes(EXT), F32)]
    return call(inject_kernel, "inject", (first_x, rec, res), outs, scalars=1, **kw)


def wave(first_x, aperture, cur, cour, fwd, begun, second, third, outer, inner, **kw):
    return call(
        wave_kernel, "wave",
        (first_x, aperture, cur, cour, fwd, begun, second, third, outer, inner, ALONG_Z, ALONG_Y),
        [((4, 4, 8, 8, NZ), F32), (planes(EXT), F32), (planes(EXT), F32)],
        [pltpu.VMEM(planes(n), F32) for n in (16, 8, 8, 8, 24)]
        + [pltpu.VMEM(fwd.shape, BF16), pltpu.SemaphoreType.DMA(())],
        scalars=2, stay=(4,), **kw,
    )


def decode(pieces, latent, **kw):
    return call(
        decode_kernel, "decode", (pieces, SPREAD, latent, PLACE, PICK),
        [((32, 8 * NZ), F32), ((16, 4, 128), F32)], **kw,
    )


def latent_rows(latent):
    return latent.reshape(8, 2, 32, NZ).transpose(1, 2, 0, 3).reshape(64, 8 * NZ)


def mixing(weight):
    taps = weight.reshape(32, 2, 2, 2, 2).transpose(0, 1, 4, 2, 3)
    same = np.eye(2, dtype=np.float32)[None, :, None, None, None, :, None]
    return (taps[:, None, :, :, :, None, :] * same).reshape(64, 32)


def latent_out(mix, taps, **kw):
    flat = call(latent_kernel, "latent", (mix, taps), [((512, NZ), F32)], **kw)[0]
    return flat.reshape(8, 32, 2, NZ).transpose(0, 2, 1, 3).reshape(8, 2, 4096)


def swaps(lower):
    return [pair for i in lower for pair in ((i, i + 1), (i + 1, i))]


def body(wave_now, wave_prev, courant, forward, receivers, residual, aperture, latent, weight):
    first_x = (lax.axis_index(SLAB) * EXT).astype(jnp.int32).reshape(1)
    cur, prev = wave_now[0], wave_prev[0]
    rec, res = receivers.transpose(1, 0, 2), residual.transpose(1, 0, 2)
    outer, inner, begun = head(first_x, cur, prev, courant, rec, res)
    count = lax.axis_size(SLAB)
    outer = lax.ppermute(outer, SLAB, swaps(range(1, count - 1, 2)))
    inner = lax.ppermute(inner, SLAB, swaps(range(0, count, 2)))
    second, third = inject(first_x, rec, res)
    lat = latent_rows(latent)
    mix = mixing(weight)
    rows, after, before = wave(
        first_x, aperture, cur, courant, forward[0], begun, second, third, outer, inner
    )
    near = lax.all_to_all(rows, "y", 0, 0, tiled=True).sum(0)
    pieces = lax.all_to_all(near, "zh", 0, 0, tiled=True)
    taps, shares = decode(pieces, lat)
    shares = lax.all_to_all(shares, ("zh", "zl"), 0, 0, tiled=True)
    shares = call(share_kernel, "share", (shares,), [((32, 4, 128), F32)])[0]
    shares = lax.all_to_all(shares, ("y", "x", "c"), 0, 0, tiled=True)
    latent_grad = latent_out(mix, taps)

    def last(pieces, out):
        final_kernel(pieces, out, scale=1.0 / math.sqrt(256 * 32 * 64))

    weight_grad = call(last, "total", (shares,), [((8, 64), F32)])[0].T
    return (after[None], before[None], latent_grad, weight_grad)


def solution(mesh):
    fine = Mesh(mesh.devices.reshape(4, 4, 4, 4, 2), PARTS)
    return jax.shard_map(
        body,
        mesh=fine,
        in_specs=(
            P(SHOT, SLAB, None, None),
            P(SHOT, SLAB, None, None),
            P(SLAB, None, None),
            P(SHOT, None, SLAB, None, None),
            P(SHOT, None, None),
            P(SHOT, None, None),
            P(SHOT, None),
            P(SLAB, SHOT, None),
            P(),
        ),
        out_specs=(
            P(SHOT, SLAB, None, None),
            P(SHOT, SLAB, None, None),
            P(SLAB, SHOT, None),
            P(),
        ),
        check_vma=False,
    )
```

```python
import math

import jax
import jax.numpy as jnp
import numpy as np
from jax import lax
from jax.experimental import pallas as pl
from jax.experimental.pallas import tpu as pltpu
from jax.sharding import Mesh, PartitionSpec as P

STEPS = 3
PARTS = ("zh", "y", "zl", "x", "c")
SHOT = ("zh", "y")
SLAB = ("zl", "x", "c")
EXT = 16
NY = 64
NZ = 128
F32 = jnp.float32
BF16 = jnp.bfloat16

stencil_weights = (-205.0 / 72.0, 8.0 / 5.0, -1.0 / 5.0, 8.0 / 315.0, -1.0 / 560.0)


def high_low(values):
    high = values.astype(BF16)
    return high, (values - high.astype(np.float32)).astype(BF16)


def band(size, center):
    out = np.zeros((size, size), np.float32)
    for k in range(5):
        for i in range(size - k):
            value = center if k == 0 else stencil_weights[k]
            out[i, i + k] = value
            out[i + k, i] = value
    return out


def constants():
    zh, zl = high_low(band(NZ, 3.0 * stencil_weights[0]))
    yh, yl = high_low(band(NY, 0.0))
    along_z = np.concatenate([zh, zh, zl], axis=0)
    along_y = np.concatenate([yh, yh, yl], axis=1)
    spread = np.zeros((NZ, 2, 2, 2, NZ // 2), np.float32)
    for k in range(NZ // 2):
        for c in range(2):
            for h in range(2):
                spread[2 * k + c, h, c, h, k] = 1.0
    spread = spread.reshape(NZ, 4 * NZ).astype(BF16)
    place = np.zeros((2, 64, 128), np.float32)
    for h in range(2):
        for j in range(2):
            for t in range(32):
                place[h, 32 * j + t, 2 * t + h] = 1.0
                place[h, 32 * j + t, 64 + 2 * t + h] = 1.0
    pick = np.zeros((8, 32), np.float32)
    for row in range(32):
        c, a, b = (row >> 3) & 1, (row >> 2) & 1, row & 1
        pick[4 * a + 2 * b + c, row] = 1.0
    return along_z, along_y, spread, place, pick


ALONG_Z, ALONG_Y, SPREAD, PLACE, PICK = constants()


def flat_laplace(planes, along_z, along_y):
    count = len(planes)
    high = [u.astype(BF16) for u in planes]
    low = [(u - h.astype(F32)).astype(BF16) for u, h in zip(planes, high)]
    rows_h, rows_l = jnp.concatenate(high, axis=0), jnp.concatenate(low, axis=0)
    z_part = jnp.dot(
        jnp.concatenate([rows_h, rows_l, rows_h], axis=1), along_z, preferred_element_type=F32
    )
    wide_h, wide_l = jnp.concatenate(high, axis=1), jnp.concatenate(low, axis=1)
    y_part = jnp.dot(
        along_y, jnp.concatenate([wide_h, wide_l, wide_h], axis=0), preferred_element_type=F32
    )
    return [z_part[NY * e : NY * (e + 1)] + y_part[:, NZ * e : NZ * (e + 1)] for e in range(count)]


def across(get, at):
    total = stencil_weights[1] * (get(at + 1) + get(at - 1))
    for k in range(2, 5):
        total = total + stencil_weights[k] * (get(at + k) + get(at - k))
    return total


def three_parts(v):
    high = v.astype(BF16)
    rest = v - high.astype(F32)
    mid = rest.astype(BF16)
    low = (rest - mid.astype(F32)).astype(BF16)
    return high, mid, low


def two_parts(v):
    high = v.astype(BF16)
    return high, (v - high.astype(F32)).astype(BF16)


def injected(rec, res, first_x, start, planes, steps):
    local = rec[0] - first_x - start
    valid = (local >= 0) & (local < planes)
    row = jnp.where(valid, local * NY + rec[1], -1)
    count = rec.shape[2]
    cells = lax.broadcasted_iota(jnp.int32, (planes * NY, count), 0)
    rows = jnp.where(cells == row, 1.0, 0.0).astype(BF16)
    depth = lax.broadcasted_iota(jnp.int32, (NZ, count), 0)
    at_depth = depth == rec[2]
    out = []
    for t in steps:
        value = jnp.where(at_depth, res[t], 0.0)
        total = None
        for part in three_parts(value):
            piece = lax.dot_general(
                rows, part, (((1,), (1,)), ((), ())), preferred_element_type=F32
            )
            total = piece if total is None else total + piece
        out.append(total)
    return out


def head_kernel(
    first_x, cur_in, prev_in, cour_in, rec_in, res_in, z_in, y_in, outer, inner, begun,
    cur, prev, cour, rec, res, along_z, along_y, sems,
):
    copies = [
        pltpu.make_async_copy(source, target, sems.at[k])
        for k, (source, target) in enumerate(
            (
                (rec_in, rec),
                (res_in, res),
                (cur_in, cur.at[4:20]),
                (z_in, along_z),
                (y_in, along_y),
                (prev_in, prev),
                (cour_in, cour),
            )
        )
    ]
    for copy in copies:
        copy.start()
    zero = jnp.zeros((4, NY, NZ), F32)
    cur[0:4] = zero
    cur[20:24] = zero
    copies[0].wait()
    copies[1].wait()
    (added,) = injected(rec[...], res[...], first_x[0], 0, EXT, (0,))
    for copy in copies[2:]:
        copy.wait()
    tz, ty = along_z[...], along_y[...]
    for group in range(0, EXT, 4):
        flat = flat_laplace([cur[group + e + 4] for e in range(4)], tz, ty)
        for e in range(4):
            i = group + e
            lap = flat[e] + across(lambda at: cur[at + 4], i)
            value = 2.0 * cur[i + 4] - prev[i] + cour[i] * lap
            begun[i] = value + added[NY * i : NY * (i + 1)]
    odd = (first_x[0] >> 4) & 1
    for message, side in ((outer, odd), (inner, 1 - odd)):
        message[0:8] = begun[pl.ds(8 * side, 8)]
        message[8:12] = cur[pl.ds(4 + 12 * side, 4)]
        message[12:16] = cour[pl.ds(12 * side, 4)]


def inject_kernel(first_x, rec, res, second, third):
    one, two = injected(rec[...], res[...], first_x[0], -4, EXT + 8, (1, 2))
    second[...] = one.reshape(EXT + 8, NY, NZ)
    third[...] = two.reshape(EXT + 8, NY, NZ)[4:20]


def wave_kernel(
    first_x, cur, cour, span_in, fwd_in, begun, second, third, outer, inner, along_z, along_y,
    rows, after, before, far_u, far_c, far_k, near_u, mid, fwd, span, sems,
):
    copies = [
        pltpu.make_async_copy(span_in, span, sems.at[0]),
        pltpu.make_async_copy(fwd_in, fwd, sems.at[1]),
    ]
    for copy in copies:
        copy.start()
    odd = (first_x[0] >> 4) & 1
    for message, side in ((outer, odd), (inner, 1 - odd)):
        far_u[pl.ds(8 * side, 8)] = message[0:8]
        far_c[pl.ds(4 * side, 4)] = message[8:12]
        far_k[pl.ds(4 * side, 4)] = message[12:16]

    def courant_at(i):
        return far_k[i + 4] if i < 0 else far_k[i - 12] if i >= EXT else cour[i]

    def now_at(i):
        return far_c[i + 4] if i < 0 else far_c[i - 12] if i >= EXT else cur[i]

    def step_at(i):
        if i < 0:
            return far_u[i + 8]
        if i >= EXT:
            return far_u[i - 8]
        if i < 4:
            return near_u[i]
        return near_u[i - 8] if i >= 12 else begun[i]

    def missing(i, others):
        total = None
        for k in range(1, 5):
            for at in (i - k, i + k):
                if at in others:
                    term = stencil_weights[k] * now_at(at)
                    total = term if total is None else total + term
        return courant_at(i) * total

    for i in range(4):
        near_u[i] = begun[i] + missing(i, range(-4, 0))
        near_u[i + 4] = begun[i + 12] + missing(i + 12, range(16, 20))
        far_u[i + 4] = far_u[i + 4] + missing(i - 4, range(0, 4))
        far_u[i + 8] = far_u[i + 8] + missing(i + 16, range(12, 16))
    tz, ty = along_z[...], along_y[...]
    for group in range(-4, EXT + 4, 8):
        flat = flat_laplace([step_at(group + e) for e in range(8)], tz, ty)
        for e in range(8):
            i = group + e
            lap = flat[e] + across(step_at, i)
            value = 2.0 * step_at(i) - now_at(i) + courant_at(i) * lap + second[i + 4]
            mid[i + 4] = value
            if 0 <= i < EXT:
                before[i] = value
    for copy in copies:
        copy.wait()
    lower = lax.broadcasted_iota(jnp.int32, (NY, NZ), 0) % 8 < 4
    for group in range(0, EXT, 4):
        flat = flat_laplace([mid[group + e + 4] for e in range(4)], tz, ty)
        images = []
        for e in range(4):
            i = group + e
            lap = flat[e] + across(lambda at: mid[at + 4], i)
            value = 2.0 * mid[i + 4] - step_at(i) + cour[i] * lap + third[i]
            after[i] = value
            acc = step_at(i) * fwd[0, i].astype(F32)
            acc = acc + mid[i + 4] * fwd[1, i].astype(F32)
            acc = acc + value * fwd[2, i].astype(F32)
            at = first_x[0] + i
            inside = (at >= span[0, 0]) & (at < span[0, 1])
            images.append(jnp.where(inside, cour[i] * acc, 0.0))
        for p in range(2):
            first, next_one = images[2 * p : 2 * p + 2]
            even = jnp.where(lower, first, pltpu.roll(next_one, 4, 0)).reshape(4, 2, 8, NZ)
            odds = jnp.where(lower, pltpu.roll(first, NY - 4, 0), next_one).reshape(4, 2, 8, NZ)
            for far in range(4):
                for half in range(2):
                    rows[2 * half, far, group // 2 + p] = even[far, half]
                    rows[2 * half + 1, far, group // 2 + p] = odds[far, half]


def decode_kernel(pieces, spread, latent, place, pick, taps, shares):
    tile = ((pieces[0] + pieces[1]) + (pieces[2] + pieces[3])).reshape(64, NZ)
    wide = None
    for part in two_parts(tile):
        piece = jnp.dot(part, spread[...], preferred_element_type=F32)
        wide = piece if wide is None else wide + piece
    for i in range(8):
        for block in range(4):
            taps[8 * block : 8 * block + 8, NZ * i : NZ * (i + 1)] = wide[
                8 * i : 8 * i + 8, NZ * block : NZ * (block + 1)
            ]
    grad = None
    for part in two_parts(taps[...]):
        piece = lax.dot_general(
            part, latent[...], (((1,), (1,)), ((), ())), preferred_element_type=F32
        )
        grad = piece if grad is None else grad + piece
    tap_j = (lax.broadcasted_iota(jnp.int32, (32, 64), 0) >> 1) & 1
    lane_j = lax.broadcasted_iota(jnp.int32, (32, 64), 1) >> 5
    grad = jnp.where(tap_j == lane_j, grad, 0.0)
    exact = dict(preferred_element_type=F32, precision=lax.Precision.HIGHEST)
    moved = jnp.concatenate(
        [jnp.dot(grad[:16], place[0], **exact), jnp.dot(grad[16:], place[1], **exact)], axis=0
    )
    total = jnp.dot(pick[...], moved, **exact)
    left = lax.broadcasted_iota(jnp.int32, (4, 128), 1) < 64
    packed = jnp.where(left, total[0:4], total[4:8])
    shares[...] = jnp.broadcast_to(packed[None], shares.shape)


def near_kernel(pieces, out):
    out[...] = (pieces[0] + pieces[1]) + (pieces[2] + pieces[3])


def store_kernel(one, two, one_out, two_out, sems):
    copies = [
        pltpu.make_async_copy(one, one_out, sems.at[0]),
        pltpu.make_async_copy(two, two_out, sems.at[1]),
    ]
    for copy in copies:
        copy.start()
    for copy in copies:
        copy.wait()


def latent_kernel(mix, taps, out):
    wide = jnp.dot(
        mix[...], taps[...], preferred_element_type=F32, precision=lax.Precision.HIGHEST
    )
    for i in range(8):
        out[64 * i : 64 * (i + 1)] = wide[:, NZ * i : NZ * (i + 1)]


def share_kernel(pieces, shares):
    total = jnp.sum(pieces[...], axis=0, keepdims=True)
    shares[...] = jnp.broadcast_to(total, shares.shape)


def final_kernel(pieces, out, *, scale):
    total = jnp.sum(pieces[...], axis=0) * scale
    out[0:4] = total[:, :64]
    out[4:8] = total[:, 64:]


VM = pl.BlockSpec(memory_space=pltpu.VMEM)
SM = pl.BlockSpec(memory_space=pltpu.SMEM)


HB = pl.BlockSpec(memory_space=pltpu.HBM)


def call(kernel, name, args, outs, scratch=(), scalars=0, stay=(), near=(), far=(), interpret=False):
    specs = [SM] * scalars + [VM] * (len(args) - scalars)
    args = list(args)
    for k in stay:
        specs[k] = HB
        if not interpret:
            args[k] = pltpu.with_memory_space_constraint(jnp.asarray(args[k]), pltpu.HBM)
    return pl.pallas_call(
        kernel,
        name=name,
        in_specs=specs,
        out_specs=[HB if k in far else VM for k in range(len(outs))],
        out_shape=[
            pltpu.VMEM(*o) if k in near and not interpret else jax.ShapeDtypeStruct(*o)
            for k, o in enumerate(outs)
        ],
        scratch_shapes=list(scratch),
        compiler_params=pltpu.CompilerParams(vmem_limit_bytes=16 << 20),
        interpret=interpret,
    )(*args)


def planes(count):
    return (count, NY, NZ)


def head(first_x, cur, prev, cour, rec, res, **kw):
    return call(
        head_kernel, "head", (first_x, cur, prev, cour, rec, res, ALONG_Z, ALONG_Y),
        [(planes(EXT), F32)] * 3,
        [
            pltpu.VMEM(planes(EXT + 8), F32), pltpu.VMEM(planes(EXT), F32),
            pltpu.VMEM(planes(EXT), F32), pltpu.VMEM(rec.shape, jnp.int32),
            pltpu.VMEM(res.shape, F32), pltpu.VMEM(ALONG_Z.shape, BF16),
            pltpu.VMEM(ALONG_Y.shape, BF16), pltpu.SemaphoreType.DMA((7,)),
        ],
        scalars=1, stay=range(1, 8), **kw,
    )


def inject(first_x, rec, res, **kw):
    outs = [(planes(EXT + 8), F32), (planes(EXT), F32)]
    return call(inject_kernel, "inject", (first_x, rec, res), outs, scalars=1, **kw)


def wave(first_x, cur, cour, aperture, fwd, begun, second, third, outer, inner, **kw):
    return call(
        wave_kernel, "wave",
        (first_x, cur, cour, aperture, fwd, begun, second, third, outer, inner, ALONG_Z, ALONG_Y),
        [((4, 4, 8, 8, NZ), F32), (planes(EXT), F32), (planes(EXT), F32)],
        [pltpu.VMEM(planes(n), F32) for n in (16, 8, 8, 8, 24)]
        + [
            pltpu.VMEM(fwd.shape, BF16), pltpu.SMEM((1, 2), jnp.int32),
            pltpu.SemaphoreType.DMA((2,)),
        ],
        scalars=1, stay=(3, 4), near=(0, 1, 2), **kw,
    )


def gather_sum(pieces, **kw):
    return call(near_kernel, "near", (pieces,), [(pieces.shape[1:], F32)], **kw)[0]


def store(one, two, **kw):
    outs = [(one.shape, F32), (two.shape, F32)]
    sems = [pltpu.SemaphoreType.DMA((2,))]
    return call(store_kernel, "store", (one, two), outs, sems, far=(0, 1), **kw)


def decode(pieces, latent, **kw):
    return call(
        decode_kernel, "decode", (pieces, SPREAD, latent, PLACE, PICK),
        [((32, 8 * NZ), F32), ((32, 4, 128), F32)], **kw,
    )


def latent_rows(latent):
    return latent.reshape(8, 2, 32, NZ).transpose(1, 2, 0, 3).reshape(64, 8 * NZ)


def mixing(weight):
    taps = weight.reshape(32, 2, 2, 2, 2).transpose(0, 1, 4, 2, 3)
    same = np.eye(2, dtype=np.float32)[None, :, None, None, None, :, None]
    return (taps[:, None, :, :, :, None, :] * same).reshape(64, 32)


def latent_out(mix, taps, **kw):
    flat = call(latent_kernel, "latent", (mix, taps), [((512, NZ), F32)], **kw)[0]
    return flat.reshape(8, 32, 2, NZ).transpose(0, 2, 1, 3).reshape(8, 2, 4096)


def swaps(lower):
    return [pair for i in lower for pair in ((i, i + 1), (i + 1, i))]


def body(wave_now, wave_prev, courant, forward, receivers, residual, aperture, latent, weight):
    first_x = (lax.axis_index(SLAB) * EXT).astype(jnp.int32).reshape(1)
    cur, prev = wave_now[0], wave_prev[0]
    rec, res = receivers.transpose(1, 0, 2), residual.transpose(1, 0, 2)
    outer, inner, begun = head(first_x, cur, prev, courant, rec, res)
    count = lax.axis_size(SLAB)
    outer = lax.ppermute(outer, SLAB, swaps(range(1, count - 1, 2)))
    inner = lax.ppermute(inner, SLAB, swaps(range(0, count, 2)))
    second, third = inject(first_x, rec, res)
    lat = latent_rows(latent)
    mix = mixing(weight)
    rows, after, before = wave(
        first_x, cur, courant, aperture, forward[0], begun, second, third, outer, inner
    )
    near = gather_sum(lax.all_to_all(rows, "y", 0, 0, tiled=True))
    pieces = lax.all_to_all(near, "zh", 0, 0, tiled=True)
    after, before = store(after, before)
    pieces, after, before, lat, mix = lax.optimization_barrier((pieces, after, before, lat, mix))
    taps, shares = decode(pieces, lat)
    latent_grad = latent_out(mix, taps)
    shares = lax.all_to_all(shares, ("y", "x", "c"), 0, 0, tiled=True)
    shares, latent_grad = lax.optimization_barrier((shares, latent_grad))
    shares = call(share_kernel, "share", (shares,), [((16, 4, 128), F32)])[0]
    shares = lax.all_to_all(shares, ("zh", "zl"), 0, 0, tiled=True)

    def last(pieces, out):
        final_kernel(pieces, out, scale=1.0 / math.sqrt(256 * 32 * 64))

    weight_grad = call(last, "total", (shares,), [((8, 64), F32)])[0].T
    return (after[None], before[None], latent_grad, weight_grad)


def solution(mesh):
    fine = Mesh(mesh.devices.reshape(4, 4, 4, 4, 2), PARTS)
    return jax.shard_map(
        body,
        mesh=fine,
        in_specs=(
            P(SHOT, SLAB, None, None),
            P(SHOT, SLAB, None, None),
            P(SLAB, None, None),
            P(SHOT, None, SLAB, None, None),
            P(SHOT, None, None),
            P(SHOT, None, None),
            P(SHOT, None),
            P(SLAB, SHOT, None),
            P(),
        ),
        out_specs=(
            P(SHOT, SLAB, None, None),
            P(SHOT, SLAB, None, None),
            P(SLAB, SHOT, None),
            P(),
        ),
        check_vma=False,
    )
```

```python
import math

import jax
import jax.numpy as jnp
import numpy as np
from jax import lax
from jax.experimental import pallas as pl
from jax.experimental.pallas import tpu as pltpu
from jax.sharding import Mesh, PartitionSpec as P

STEPS = 3
PARTS = ("zh", "y", "zl", "x", "c")
SHOT = ("zh", "y")
SLAB = ("zl", "x", "c")
EXT = 16
NY = 64
NZ = 128
F32 = jnp.float32
BF16 = jnp.bfloat16

stencil_weights = (-205.0 / 72.0, 8.0 / 5.0, -1.0 / 5.0, 8.0 / 315.0, -1.0 / 560.0)


def high_low(values):
    high = values.astype(BF16)
    return high, (values - high.astype(np.float32)).astype(BF16)


def band(size, center):
    out = np.zeros((size, size), np.float32)
    for k in range(5):
        for i in range(size - k):
            value = center if k == 0 else stencil_weights[k]
            out[i, i + k] = value
            out[i + k, i] = value
    return out


def constants():
    zh, zl = high_low(band(NZ, 3.0 * stencil_weights[0]))
    yh, yl = high_low(band(NY, 0.0))
    along_z = np.concatenate([zh, zh, zl], axis=0)
    along_y = np.concatenate([yh, yh, yl], axis=1)
    spread = np.zeros((NZ, 2, 2, 2, NZ // 2), np.float32)
    for k in range(NZ // 2):
        for c in range(2):
            for h in range(2):
                spread[2 * k + c, h, c, h, k] = 1.0
    spread = spread.reshape(NZ, 4 * NZ).astype(BF16)
    pick = np.zeros((8, 16), np.float32)
    for row in range(16):
        c, a, b = (row >> 3) & 1, (row >> 2) & 1, row & 1
        pick[4 * a + 2 * b + c, row] = 1.0
    return along_z, along_y, spread, pick


ALONG_Z, ALONG_Y, SPREAD, PICK = constants()


def flat_laplace(planes, along_z, along_y):
    count = len(planes)
    high = [u.astype(BF16) for u in planes]
    low = [(u - h.astype(F32)).astype(BF16) for u, h in zip(planes, high)]
    rows_h, rows_l = jnp.concatenate(high, axis=0), jnp.concatenate(low, axis=0)
    z_part = jnp.dot(
        jnp.concatenate([rows_h, rows_l, rows_h], axis=1), along_z, preferred_element_type=F32
    )
    wide_h, wide_l = jnp.concatenate(high, axis=1), jnp.concatenate(low, axis=1)
    y_part = jnp.dot(
        along_y, jnp.concatenate([wide_h, wide_l, wide_h], axis=0), preferred_element_type=F32
    )
    return [z_part[NY * e : NY * (e + 1)] + y_part[:, NZ * e : NZ * (e + 1)] for e in range(count)]


def across(get, at):
    total = stencil_weights[1] * (get(at + 1) + get(at - 1))
    for k in range(2, 5):
        total = total + stencil_weights[k] * (get(at + k) + get(at - k))
    return total


def three_parts(v):
    high = v.astype(BF16)
    rest = v - high.astype(F32)
    mid = rest.astype(BF16)
    low = (rest - mid.astype(F32)).astype(BF16)
    return high, mid, low


def two_parts(v):
    high = v.astype(BF16)
    return high, (v - high.astype(F32)).astype(BF16)


def injected(rec, res, first_x, start, planes, steps):
    local = rec[0] - first_x - start
    valid = (local >= 0) & (local < planes)
    row = jnp.where(valid, local * NY + rec[1], -1)
    count = rec.shape[2]
    cells = lax.broadcasted_iota(jnp.int32, (planes * NY, count), 0)
    rows = jnp.where(cells == row, 1.0, 0.0).astype(BF16)
    depth = lax.broadcasted_iota(jnp.int32, (NZ, count), 0)
    at_depth = depth == rec[2]
    out = []
    for t in steps:
        value = jnp.where(at_depth, res[t], 0.0)
        total = None
        for part in three_parts(value):
            piece = lax.dot_general(
                rows, part, (((1,), (1,)), ((), ())), preferred_element_type=F32
            )
            total = piece if total is None else total + piece
        out.append(total)
    return out


def head_kernel(
    first_x, cur_in, prev_in, cour_in, rec_in, res_in, z_in, y_in, outer, inner, begun,
    cur, prev, cour, rec, res, along_z, along_y, sems,
):
    copies = [
        pltpu.make_async_copy(source, target, sems.at[k])
        for k, (source, target) in enumerate(
            (
                (rec_in, rec),
                (res_in, res),
                (cur_in, cur.at[4:20]),
                (z_in, along_z),
                (y_in, along_y),
                (prev_in, prev),
                (cour_in, cour),
            )
        )
    ]
    for copy in copies:
        copy.start()
    zero = jnp.zeros((4, NY, NZ), F32)
    cur[0:4] = zero
    cur[20:24] = zero
    copies[0].wait()
    copies[1].wait()
    (added,) = injected(rec[...], res[...], first_x[0], 0, EXT, (0,))
    for copy in copies[2:]:
        copy.wait()
    tz, ty = along_z[...], along_y[...]
    for group in range(0, EXT, 4):
        flat = flat_laplace([cur[group + e + 4] for e in range(4)], tz, ty)
        for e in range(4):
            i = group + e
            lap = flat[e] + across(lambda at: cur[at + 4], i)
            value = 2.0 * cur[i + 4] - prev[i] + cour[i] * lap
            begun[i] = value + added[NY * i : NY * (i + 1)]
    odd = (first_x[0] >> 4) & 1
    for message, side in ((outer, odd), (inner, 1 - odd)):
        message[0:8] = begun[pl.ds(8 * side, 8)]
        message[8:12] = cur[pl.ds(4 + 12 * side, 4)]
        message[12:16] = cour[pl.ds(12 * side, 4)]


def inject_kernel(first_x, fwd_in, rec, res, second, third, fwd, sem):
    copy = pltpu.make_async_copy(fwd_in, fwd, sem)
    copy.start()
    one, two = injected(rec[...], res[...], first_x[0], -4, EXT + 8, (1, 2))
    second[...] = one.reshape(EXT + 8, NY, NZ)
    third[...] = two.reshape(EXT + 8, NY, NZ)[4:20]
    copy.wait()


def wave_kernel(
    first_x, cur, cour, span_in, fwd, begun, second, third, outer, inner, along_z, along_y,
    rows, after, before, far_u, far_c, far_k, near_u, mid, span, sem,
):
    copy = pltpu.make_async_copy(span_in, span, sem)
    copy.start()
    odd = (first_x[0] >> 4) & 1
    for message, side in ((outer, odd), (inner, 1 - odd)):
        far_u[pl.ds(8 * side, 8)] = message[0:8]
        far_c[pl.ds(4 * side, 4)] = message[8:12]
        far_k[pl.ds(4 * side, 4)] = message[12:16]

    def courant_at(i):
        return far_k[i + 4] if i < 0 else far_k[i - 12] if i >= EXT else cour[i]

    def now_at(i):
        return far_c[i + 4] if i < 0 else far_c[i - 12] if i >= EXT else cur[i]

    def step_at(i):
        if i < 0:
            return far_u[i + 8]
        if i >= EXT:
            return far_u[i - 8]
        if i < 4:
            return near_u[i]
        return near_u[i - 8] if i >= 12 else begun[i]

    def missing(i, others):
        total = None
        for k in range(1, 5):
            for at in (i - k, i + k):
                if at in others:
                    term = stencil_weights[k] * now_at(at)
                    total = term if total is None else total + term
        return courant_at(i) * total

    for i in range(4):
        near_u[i] = begun[i] + missing(i, range(-4, 0))
        near_u[i + 4] = begun[i + 12] + missing(i + 12, range(16, 20))
        far_u[i + 4] = far_u[i + 4] + missing(i - 4, range(0, 4))
        far_u[i + 8] = far_u[i + 8] + missing(i + 16, range(12, 16))
    tz, ty = along_z[...], along_y[...]
    for group in range(-4, EXT + 4, 8):
        flat = flat_laplace([step_at(group + e) for e in range(8)], tz, ty)
        for e in range(8):
            i = group + e
            lap = flat[e] + across(step_at, i)
            value = 2.0 * step_at(i) - now_at(i) + courant_at(i) * lap + second[i + 4]
            mid[i + 4] = value
            if 0 <= i < EXT:
                before[i] = value
    copy.wait()
    lower = lax.broadcasted_iota(jnp.int32, (8, 8, NZ), 1) < 4
    for group in range(0, EXT, 4):
        flat = flat_laplace([mid[group + e + 4] for e in range(4)], tz, ty)
        images = []
        for e in range(4):
            i = group + e
            lap = flat[e] + across(lambda at: mid[at + 4], i)
            value = 2.0 * mid[i + 4] - step_at(i) + cour[i] * lap + third[i]
            after[i] = value
            acc = step_at(i) * fwd[0, i].astype(F32)
            acc = acc + mid[i + 4] * fwd[1, i].astype(F32)
            acc = acc + value * fwd[2, i].astype(F32)
            at = first_x[0] + i
            inside = (at >= span[0, 0]) & (at < span[0, 1])
            images.append(jnp.where(inside, cour[i] * acc, 0.0))
        for p in range(2):
            first, next_one = (v.reshape(8, 8, NZ) for v in images[2 * p : 2 * p + 2])
            turned = pltpu.roll(next_one, 4, 1)
            even = jnp.where(lower, first, turned).reshape(4, 2, 8, NZ)
            odds = jnp.where(lower, turned, first).reshape(4, 2, 8, NZ)
            for far in range(4):
                for half in range(2):
                    rows[2 * half, far, group // 2 + p] = even[far, half]
                    rows[2 * half + 1, far, group // 2 + p] = odds[far, half]


def decode_kernel(odd_y, pieces, spread, latent, pick, tile, shares):
    total = (pieces[0] + pieces[1]) + (pieces[2] + pieces[3])
    total = jnp.where(odd_y[0] == 1, pltpu.roll(total, 4, 1), total).reshape(64, NZ)
    tile[...] = total
    wide = jnp.dot(
        jnp.concatenate(two_parts(total), axis=0), spread[...], preferred_element_type=F32
    )
    taps = jnp.concatenate(
        [
            jnp.concatenate(
                [
                    wide[64 * part + 8 * i : 64 * part + 8 * i + 8, NZ * c : NZ * (c + 1)]
                    for i in range(8)
                ],
                axis=1,
            )
            for part in range(2)
            for c in range(2)
        ],
        axis=0,
    ).astype(BF16)
    grad = lax.dot_general(
        taps, latent[...], (((1,), (1,)), ((), ())), preferred_element_type=F32
    )
    grad = grad[0:16] + grad[16:32]
    tap_j = (lax.broadcasted_iota(jnp.int32, (16, NZ), 0) >> 1) & 1
    lane_j = lax.broadcasted_iota(jnp.int32, (16, NZ), 1) >> 6
    grad = jnp.dot(
        pick[...], jnp.where(tap_j == lane_j, grad, 0.0),
        preferred_element_type=F32, precision=lax.Precision.HIGHEST,
    )
    grad = grad + pltpu.roll(grad, 64, 1)
    left = lax.broadcasted_iota(jnp.int32, (4, NZ), 1) < 64
    packed = jnp.where(left, grad[0:4], grad[4:8])
    shares[...] = jnp.broadcast_to(packed[None], shares.shape)


def near_kernel(pieces, out):
    out[...] = (pieces[0] + pieces[1]) + (pieces[2] + pieces[3])


def store_kernel(one, two, one_out, two_out, sems):
    copies = [
        pltpu.make_async_copy(one, one_out, sems.at[0]),
        pltpu.make_async_copy(two, two_out, sems.at[1]),
    ]
    for copy in copies:
        copy.start()
    for copy in copies:
        copy.wait()


def latent_kernel(mix, tile, spread, out, taps):
    wide = None
    for part in two_parts(tile[...]):
        piece = jnp.dot(part, spread[...], preferred_element_type=F32)
        wide = piece if wide is None else wide + piece
    for i in range(8):
        for block in range(4):
            taps[8 * block : 8 * block + 8, NZ * i : NZ * (i + 1)] = wide[
                8 * i : 8 * i + 8, NZ * block : NZ * (block + 1)
            ]
    mixed = jnp.dot(
        mix[...], taps[...], preferred_element_type=F32, precision=lax.Precision.HIGHEST
    )
    for i in range(8):
        out[64 * i : 64 * (i + 1)] = mixed[:, NZ * i : NZ * (i + 1)]


def share_kernel(pieces, shares):
    total = jnp.sum(pieces[...], axis=0, keepdims=True)
    shares[...] = jnp.broadcast_to(total, shares.shape)


def final_kernel(pieces, out, *, scale):
    total = jnp.sum(pieces[...], axis=0) * scale
    out[0:4] = total[:, :64]
    out[4:8] = total[:, 64:]


VM = pl.BlockSpec(memory_space=pltpu.VMEM)
SM = pl.BlockSpec(memory_space=pltpu.SMEM)


HB = pl.BlockSpec(memory_space=pltpu.HBM)


def call(kernel, name, args, outs, scratch=(), scalars=0, stay=(), near=(), far=(), interpret=False):
    specs = [SM] * scalars + [VM] * (len(args) - scalars)
    args = list(args)
    for k in stay:
        specs[k] = HB
        if not interpret:
            args[k] = pltpu.with_memory_space_constraint(jnp.asarray(args[k]), pltpu.HBM)
    return pl.pallas_call(
        kernel,
        name=name,
        in_specs=specs,
        out_specs=[HB if k in far else VM for k in range(len(outs))],
        out_shape=[
            pltpu.VMEM(*o) if k in near and not interpret else jax.ShapeDtypeStruct(*o)
            for k, o in enumerate(outs)
        ],
        scratch_shapes=list(scratch),
        compiler_params=pltpu.CompilerParams(vmem_limit_bytes=16 << 20),
        interpret=interpret,
    )(*args)


def planes(count):
    return (count, NY, NZ)


def head(first_x, cur, prev, cour, rec, res, **kw):
    return call(
        head_kernel, "head", (first_x, cur, prev, cour, rec, res, ALONG_Z, ALONG_Y),
        [(planes(EXT), F32)] * 3,
        [
            pltpu.VMEM(planes(EXT + 8), F32), pltpu.VMEM(planes(EXT), F32),
            pltpu.VMEM(planes(EXT), F32), pltpu.VMEM(rec.shape, jnp.int32),
            pltpu.VMEM(res.shape, F32), pltpu.VMEM(ALONG_Z.shape, BF16),
            pltpu.VMEM(ALONG_Y.shape, BF16), pltpu.SemaphoreType.DMA((7,)),
        ],
        scalars=1, stay=range(1, 8), near=(0, 1, 2), **kw,
    )


def inject(first_x, fwd, rec, res, **kw):
    outs = [(planes(EXT + 8), F32), (planes(EXT), F32), (fwd.shape, BF16)]
    return call(
        inject_kernel, "inject", (first_x, fwd, rec, res), outs,
        [pltpu.SemaphoreType.DMA(())], scalars=1, stay=(1,), near=(0, 1, 2), **kw,
    )


def wave(first_x, cur, cour, aperture, fwd, begun, second, third, outer, inner, **kw):
    return call(
        wave_kernel, "wave",
        (first_x, cur, cour, aperture, fwd, begun, second, third, outer, inner, ALONG_Z, ALONG_Y),
        [((4, 4, 8, 8, NZ), F32), (planes(EXT), F32), (planes(EXT), F32)],
        [pltpu.VMEM(planes(n), F32) for n in (16, 8, 8, 8, 24)]
        + [
            pltpu.SMEM((1, 2), jnp.int32), pltpu.SemaphoreType.DMA(()),
        ],
        scalars=1, stay=(3,), near=(0, 1, 2), **kw,
    )


def gather_sum(pieces, **kw):
    outs = [(pieces.shape[1:], F32)]
    return call(near_kernel, "near", (pieces,), outs, near=(0,), **kw)[0]


def store(one, two, **kw):
    outs = [(one.shape, F32), (two.shape, F32)]
    sems = [pltpu.SemaphoreType.DMA((2,))]
    return call(store_kernel, "store", (one, two), outs, sems, far=(0, 1), **kw)


def decode(odd_y, pieces, latent, **kw):
    return call(
        decode_kernel, "decode", (odd_y, pieces, SPREAD[:, : 2 * NZ], latent, PICK),
        [((64, NZ), F32), ((32, 4, NZ), F32)], scalars=1, near=(0, 1), **kw,
    )


def latent_rows(latent):
    cells = latent.reshape(8, 2, 64, NZ // 2).transpose(1, 2, 0, 3)
    return jnp.pad(cells, ((0, 0), (0, 0), (0, 0), (0, NZ // 2))).reshape(NZ, 8 * NZ)


def mixing(weight):
    taps = weight.reshape(32, 2, 2, 2, 2).transpose(0, 1, 4, 2, 3)
    same = np.eye(2, dtype=np.float32)[None, :, None, None, None, :, None]
    return (taps[:, None, :, :, :, None, :] * same).reshape(64, 32)


def latent_out(mix, tile, **kw):
    flat = call(
        latent_kernel, "latent", (mix, tile, SPREAD), [((512, NZ), F32)],
        [pltpu.VMEM((32, 8 * NZ), F32)], **kw,
    )[0]
    return flat.reshape(8, 32, 2, NZ).transpose(0, 2, 1, 3).reshape(8, 2, 4096)


def swaps(lower):
    return [pair for i in lower for pair in ((i, i + 1), (i + 1, i))]


def body(wave_now, wave_prev, courant, forward, receivers, residual, aperture, latent, weight):
    first_x = (lax.axis_index(SLAB) * EXT).astype(jnp.int32).reshape(1)
    cur, prev = wave_now[0], wave_prev[0]
    rec, res = receivers.transpose(1, 0, 2), residual.transpose(1, 0, 2)
    outer, inner, begun = head(first_x, cur, prev, courant, rec, res)
    count = lax.axis_size(SLAB)
    outer = lax.ppermute(outer, SLAB, swaps(range(1, count - 1, 2)))
    inner = lax.ppermute(inner, SLAB, swaps(range(0, count, 2)))
    second, third, fwd = inject(first_x, forward[0], rec, res)
    lat = latent_rows(latent)
    mix = mixing(weight)
    rows, after, before = wave(
        first_x, cur, courant, aperture, fwd, begun, second, third, outer, inner
    )
    near = gather_sum(lax.all_to_all(rows, "y", 0, 0, tiled=True))
    pieces = lax.all_to_all(near, "zh", 0, 0, tiled=True)
    after, before = store(after, before)
    pieces, after, before, lat, mix = lax.optimization_barrier((pieces, after, before, lat, mix))
    odd_y = (lax.axis_index("y") & 1).astype(jnp.int32).reshape(1)
    tile, shares = decode(odd_y, pieces, lat)
    latent_grad = latent_out(mix, tile)
    shares = lax.all_to_all(shares, ("y", "x", "c"), 0, 0, tiled=True)
    shares, latent_grad = lax.optimization_barrier((shares, latent_grad))
    shares = call(share_kernel, "share", (shares,), [((16, 4, 128), F32)])[0]
    shares = lax.all_to_all(shares, ("zh", "zl"), 0, 0, tiled=True)

    def last(pieces, out):
        final_kernel(pieces, out, scale=1.0 / math.sqrt(256 * 32 * 64))

    weight_grad = call(last, "total", (shares,), [((8, 64), F32)])[0].T
    return (after[None], before[None], latent_grad, weight_grad)


def solution(mesh):
    fine = Mesh(mesh.devices.reshape(4, 4, 4, 4, 2), PARTS)
    return jax.shard_map(
        body,
        mesh=fine,
        in_specs=(
            P(SHOT, SLAB, None, None),
            P(SHOT, SLAB, None, None),
            P(SLAB, None, None),
            P(SHOT, None, SLAB, None, None),
            P(SHOT, None, None),
            P(SHOT, None, None),
            P(SHOT, None),
            P(SLAB, SHOT, None),
            P(),
        ),
        out_specs=(
            P(SHOT, SLAB, None, None),
            P(SHOT, SLAB, None, None),
            P(SLAB, SHOT, None),
            P(),
        ),
        check_vma=False,
    )
```

```python
import math

import jax
import jax.numpy as jnp
import numpy as np
from jax import lax
from jax.experimental import pallas as pl
from jax.experimental.pallas import tpu as pltpu
from jax.sharding import Mesh, PartitionSpec as P

STEPS = 3
PARTS = ("zh", "y", "zl", "x", "c")
SHOT = ("zh", "y")
SLAB = ("zl", "x", "c")
EXT = 16
NY = 64
NZ = 128
F32 = jnp.float32
BF16 = jnp.bfloat16

stencil_weights = (-205.0 / 72.0, 8.0 / 5.0, -1.0 / 5.0, 8.0 / 315.0, -1.0 / 560.0)


def high_low(values):
    high = values.astype(BF16)
    return high, (values - high.astype(np.float32)).astype(BF16)


def band(size, center):
    out = np.zeros((size, size), np.float32)
    for k in range(5):
        for i in range(size - k):
            value = center if k == 0 else stencil_weights[k]
            out[i, i + k] = value
            out[i + k, i] = value
    return out


def constants():
    zh, zl = high_low(band(NZ, 3.0 * stencil_weights[0]))
    yh, yl = high_low(band(NY, 0.0))
    along_z = np.concatenate([zh, zh, zl], axis=0)
    along_y = np.concatenate([yh, yh, yl], axis=1)
    spread = np.zeros((NZ, 2, 2, 2, NZ // 2), np.float32)
    for k in range(NZ // 2):
        for c in range(2):
            for h in range(2):
                spread[2 * k + c, h, c, h, k] = 1.0
    spread = spread.reshape(NZ, 4 * NZ).astype(BF16)
    pick = np.zeros((8, 16), np.float32)
    for row in range(16):
        c, a, b = (row >> 3) & 1, (row >> 2) & 1, row & 1
        pick[4 * a + 2 * b + c, row] = 1.0
    return along_z, along_y, spread, pick


ALONG_Z, ALONG_Y, SPREAD, PICK = constants()


def flat_laplace(planes, along_z, along_y):
    count = len(planes)
    high = [u.astype(BF16) for u in planes]
    low = [(u - h.astype(F32)).astype(BF16) for u, h in zip(planes, high)]
    rows_h, rows_l = jnp.concatenate(high, axis=0), jnp.concatenate(low, axis=0)
    z_part = jnp.dot(
        jnp.concatenate([rows_h, rows_l, rows_h], axis=1), along_z, preferred_element_type=F32
    )
    wide_h, wide_l = jnp.concatenate(high, axis=1), jnp.concatenate(low, axis=1)
    y_part = jnp.dot(
        along_y, jnp.concatenate([wide_h, wide_l, wide_h], axis=0), preferred_element_type=F32
    )
    return [z_part[NY * e : NY * (e + 1)] + y_part[:, NZ * e : NZ * (e + 1)] for e in range(count)]


def across(get, at):
    total = stencil_weights[1] * (get(at + 1) + get(at - 1))
    for k in range(2, 5):
        total = total + stencil_weights[k] * (get(at + k) + get(at - k))
    return total


def three_parts(v):
    high = v.astype(BF16)
    rest = v - high.astype(F32)
    mid = rest.astype(BF16)
    low = (rest - mid.astype(F32)).astype(BF16)
    return high, mid, low


def two_parts(v):
    high = v.astype(BF16)
    return high, (v - high.astype(F32)).astype(BF16)


def slab_start():
    return lax.axis_index(SLAB) * EXT


def core():
    return lax.axis_index("c")


def odd_y():
    return lax.axis_index("y") & 1


def injected(rec, res, first_x, start, planes, steps):
    local = rec[0] - first_x - start
    valid = (local >= 0) & (local < planes)
    row = jnp.where(valid, local * NY + rec[1], -1)
    count = rec.shape[2]
    cells = lax.broadcasted_iota(jnp.int32, (planes * NY, count), 0)
    rows = jnp.where(cells == row, 1.0, 0.0).astype(BF16)
    depth = lax.broadcasted_iota(jnp.int32, (NZ, count), 0)
    at_depth = depth == rec[2]
    out = []
    for t in steps:
        value = jnp.where(at_depth, res[t], 0.0)
        total = None
        for part in three_parts(value):
            piece = lax.dot_general(
                rows, part, (((1,), (1,)), ((), ())), preferred_element_type=F32
            )
            total = piece if total is None else total + piece
        out.append(total)
    return out


def head_kernel(
    cur_in, prev_in, cour_in, rec_in, res_in, z_in, y_in, outer, inner, begun,
    cur, prev, cour, rec, res, along_z, along_y, sems,
):
    copies = [
        pltpu.make_async_copy(source, target, sems.at[k])
        for k, (source, target) in enumerate(
            (
                (rec_in, rec),
                (res_in, res),
                (cur_in, cur.at[4:20]),
                (z_in, along_z),
                (y_in, along_y),
                (prev_in, prev),
                (cour_in, cour),
            )
        )
    ]
    for copy in copies:
        copy.start()
    zero = jnp.zeros((4, NY, NZ), F32)
    cur[0:4] = zero
    cur[20:24] = zero
    copies[0].wait()
    copies[1].wait()
    (added,) = injected(rec[...], res[...], slab_start(), 0, EXT, (0,))
    for copy in copies[2:]:
        copy.wait()
    tz, ty = along_z[...], along_y[...]
    for group in range(0, EXT, 4):
        flat = flat_laplace([cur[group + e + 4] for e in range(4)], tz, ty)
        for e in range(4):
            i = group + e
            lap = flat[e] + across(lambda at: cur[at + 4], i)
            value = 2.0 * cur[i + 4] - prev[i] + cour[i] * lap
            begun[i] = value + added[NY * i : NY * (i + 1)]
    odd = core()
    for message, side in ((outer, odd), (inner, 1 - odd)):
        message[0:8] = begun[pl.ds(8 * side, 8)]
        message[8:12] = cur[pl.ds(4 + 12 * side, 4)]
        message[12:16] = cour[pl.ds(12 * side, 4)]


def inject_kernel(fwd_in, rec, res, second, third, fwd, sem):
    copy = pltpu.make_async_copy(fwd_in, fwd, sem)
    copy.start()
    one, two = injected(rec[...], res[...], slab_start(), -4, EXT + 8, (1, 2))
    second[...] = one.reshape(EXT + 8, NY, NZ)
    third[...] = two.reshape(EXT + 8, NY, NZ)[4:20]
    copy.wait()


def wave_kernel(
    cur, cour, span_in, fwd, begun, second, third, outer, inner, along_z, along_y,
    rows, after, before, far_u, far_c, far_k, near_u, mid, span, sem,
):
    first_x = slab_start()
    copy = pltpu.make_async_copy(span_in, span, sem)
    copy.start()
    odd = core()
    for message, side in ((outer, odd), (inner, 1 - odd)):
        far_u[pl.ds(8 * side, 8)] = message[0:8]
        far_c[pl.ds(4 * side, 4)] = message[8:12]
        far_k[pl.ds(4 * side, 4)] = message[12:16]

    def courant_at(i):
        return far_k[i + 4] if i < 0 else far_k[i - 12] if i >= EXT else cour[i]

    def now_at(i):
        return far_c[i + 4] if i < 0 else far_c[i - 12] if i >= EXT else cur[i]

    def step_at(i):
        if i < 0:
            return far_u[i + 8]
        if i >= EXT:
            return far_u[i - 8]
        if i < 4:
            return near_u[i]
        return near_u[i - 8] if i >= 12 else begun[i]

    def missing(i, others):
        total = None
        for k in range(1, 5):
            for at in (i - k, i + k):
                if at in others:
                    term = stencil_weights[k] * now_at(at)
                    total = term if total is None else total + term
        return courant_at(i) * total

    for i in range(4):
        near_u[i] = begun[i] + missing(i, range(-4, 0))
        near_u[i + 4] = begun[i + 12] + missing(i + 12, range(16, 20))
        far_u[i + 4] = far_u[i + 4] + missing(i - 4, range(0, 4))
        far_u[i + 8] = far_u[i + 8] + missing(i + 16, range(12, 16))
    tz, ty = along_z[...], along_y[...]
    for group in range(-4, EXT + 4, 8):
        flat = flat_laplace([step_at(group + e) for e in range(8)], tz, ty)
        for e in range(8):
            i = group + e
            lap = flat[e] + across(step_at, i)
            value = 2.0 * step_at(i) - now_at(i) + courant_at(i) * lap + second[i + 4]
            mid[i + 4] = value
            if 0 <= i < EXT:
                before[i] = value
    copy.wait()
    lower = lax.broadcasted_iota(jnp.int32, (8, 8, NZ), 1) < 4
    for group in range(0, EXT, 4):
        flat = flat_laplace([mid[group + e + 4] for e in range(4)], tz, ty)
        images = []
        for e in range(4):
            i = group + e
            lap = flat[e] + across(lambda at: mid[at + 4], i)
            value = 2.0 * mid[i + 4] - step_at(i) + cour[i] * lap + third[i]
            after[i] = value
            acc = step_at(i) * fwd[0, i].astype(F32)
            acc = acc + mid[i + 4] * fwd[1, i].astype(F32)
            acc = acc + value * fwd[2, i].astype(F32)
            at = first_x + i
            inside = (at >= span[0, 0]) & (at < span[0, 1])
            images.append(jnp.where(inside, cour[i] * acc, 0.0))
        for p in range(2):
            first, next_one = (v.reshape(8, 8, NZ) for v in images[2 * p : 2 * p + 2])
            turned = pltpu.roll(next_one, 4, 1)
            even = jnp.where(lower, first, turned).reshape(4, 2, 8, NZ)
            odds = jnp.where(lower, turned, first).reshape(4, 2, 8, NZ)
            for far in range(4):
                for half in range(2):
                    rows[2 * half, far, group // 2 + p] = even[far, half]
                    rows[2 * half + 1, far, group // 2 + p] = odds[far, half]


def decode_kernel(pieces, spread, latent, pick, tile, shares):
    total = (pieces[0] + pieces[1]) + (pieces[2] + pieces[3])
    total = jnp.where(odd_y() == 1, pltpu.roll(total, 4, 1), total).reshape(64, NZ)
    tile[...] = total
    wide = jnp.dot(
        jnp.concatenate(two_parts(total), axis=0), spread[...], preferred_element_type=F32
    )
    taps = jnp.concatenate(
        [
            jnp.concatenate(
                [
                    wide[64 * part + 8 * i : 64 * part + 8 * i + 8, NZ * c : NZ * (c + 1)]
                    for i in range(8)
                ],
                axis=1,
            )
            for part in range(2)
            for c in range(2)
        ],
        axis=0,
    ).astype(BF16)
    grad = lax.dot_general(
        taps, latent[...], (((1,), (1,)), ((), ())), preferred_element_type=F32
    )
    grad = grad[0:16] + grad[16:32]
    tap_j = (lax.broadcasted_iota(jnp.int32, (16, NZ), 0) >> 1) & 1
    lane_j = lax.broadcasted_iota(jnp.int32, (16, NZ), 1) >> 6
    grad = jnp.dot(
        pick[...], jnp.where(tap_j == lane_j, grad, 0.0),
        preferred_element_type=F32, precision=lax.Precision.HIGHEST,
    )
    grad = grad + pltpu.roll(grad, 64, 1)
    left = lax.broadcasted_iota(jnp.int32, (4, NZ), 1) < 64
    packed = jnp.where(left, grad[0:4], grad[4:8])
    shares[...] = jnp.broadcast_to(packed[None], shares.shape)


def near_kernel(pieces, out):
    out[...] = (pieces[0] + pieces[1]) + (pieces[2] + pieces[3])


def store_kernel(one, two, one_out, two_out, sems):
    copies = [
        pltpu.make_async_copy(one, one_out, sems.at[0]),
        pltpu.make_async_copy(two, two_out, sems.at[1]),
    ]
    for copy in copies:
        copy.start()
    for copy in copies:
        copy.wait()


def latent_kernel(mix, tile, spread, out, taps):
    wide = None
    for part in two_parts(tile[...]):
        piece = jnp.dot(part, spread[...], preferred_element_type=F32)
        wide = piece if wide is None else wide + piece
    for i in range(8):
        for block in range(4):
            taps[8 * block : 8 * block + 8, NZ * i : NZ * (i + 1)] = wide[
                8 * i : 8 * i + 8, NZ * block : NZ * (block + 1)
            ]
    mixed = jnp.dot(
        mix[...], taps[...], preferred_element_type=F32, precision=lax.Precision.HIGHEST
    )
    for i in range(8):
        out[64 * i : 64 * (i + 1)] = mixed[:, NZ * i : NZ * (i + 1)]


def share_kernel(pieces, shares):
    total = jnp.sum(pieces[...], axis=0, keepdims=True)
    shares[...] = jnp.broadcast_to(total, shares.shape)


def final_kernel(pieces, out, *, scale):
    total = jnp.sum(pieces[...], axis=0) * scale
    out[0:4] = total[:, :64]
    out[4:8] = total[:, 64:]


VM = pl.BlockSpec(memory_space=pltpu.VMEM)


HB = pl.BlockSpec(memory_space=pltpu.HBM)


def call(kernel, name, args, outs, scratch=(), stay=(), near=(), far=(), interpret=False):
    specs = [VM] * len(args)
    args = list(args)
    for k in stay:
        specs[k] = HB
        if not interpret:
            args[k] = pltpu.with_memory_space_constraint(jnp.asarray(args[k]), pltpu.HBM)
    return pl.pallas_call(
        kernel,
        name=name,
        in_specs=specs,
        out_specs=[HB if k in far else VM for k in range(len(outs))],
        out_shape=[
            pltpu.VMEM(*o) if k in near and not interpret else jax.ShapeDtypeStruct(*o)
            for k, o in enumerate(outs)
        ],
        scratch_shapes=list(scratch),
        compiler_params=pltpu.CompilerParams(vmem_limit_bytes=16 << 20),
        interpret=interpret,
    )(*args)


def planes(count):
    return (count, NY, NZ)


def head(cur, prev, cour, rec, res, **kw):
    return call(
        head_kernel, "head", (cur, prev, cour, rec, res, ALONG_Z, ALONG_Y),
        [(planes(EXT), F32)] * 3,
        [
            pltpu.VMEM(planes(EXT + 8), F32), pltpu.VMEM(planes(EXT), F32),
            pltpu.VMEM(planes(EXT), F32), pltpu.VMEM(rec.shape, jnp.int32),
            pltpu.VMEM(res.shape, F32), pltpu.VMEM(ALONG_Z.shape, BF16),
            pltpu.VMEM(ALONG_Y.shape, BF16), pltpu.SemaphoreType.DMA((7,)),
        ],
        stay=range(7), near=(0, 1, 2), **kw,
    )


def inject(fwd, rec, res, **kw):
    outs = [(planes(EXT + 8), F32), (planes(EXT), F32), (fwd.shape, BF16)]
    return call(
        inject_kernel, "inject", (fwd, rec, res), outs,
        [pltpu.SemaphoreType.DMA(())], stay=(0,), near=(0, 1, 2), **kw,
    )


def wave(cur, cour, aperture, fwd, begun, second, third, outer, inner, **kw):
    return call(
        wave_kernel, "wave",
        (cur, cour, aperture, fwd, begun, second, third, outer, inner, ALONG_Z, ALONG_Y),
        [((4, 4, 8, 8, NZ), F32), (planes(EXT), F32), (planes(EXT), F32)],
        [pltpu.VMEM(planes(n), F32) for n in (16, 8, 8, 8, 24)]
        + [
            pltpu.SMEM((1, 2), jnp.int32), pltpu.SemaphoreType.DMA(()),
        ],
        stay=(2,), near=(0, 1, 2), **kw,
    )


def gather_sum(pieces, **kw):
    outs = [(pieces.shape[1:], F32)]
    return call(near_kernel, "near", (pieces,), outs, near=(0,), **kw)[0]


def store(one, two, **kw):
    outs = [(one.shape, F32), (two.shape, F32)]
    sems = [pltpu.SemaphoreType.DMA((2,))]
    return call(store_kernel, "store", (one, two), outs, sems, far=(0, 1), **kw)


def decode(pieces, latent, **kw):
    return call(
        decode_kernel, "decode", (pieces, SPREAD[:, : 2 * NZ], latent, PICK),
        [((64, NZ), F32), ((32, 4, NZ), F32)], near=(0, 1), **kw,
    )


def latent_rows(latent):
    cells = latent.reshape(8, 2, 64, NZ // 2).transpose(1, 2, 0, 3)
    return jnp.pad(cells, ((0, 0), (0, 0), (0, 0), (0, NZ // 2))).reshape(NZ, 8 * NZ)


def mixing(weight):
    taps = weight.reshape(32, 2, 2, 2, 2).transpose(0, 1, 4, 2, 3)
    same = np.eye(2, dtype=np.float32)[None, :, None, None, None, :, None]
    return (taps[:, None, :, :, :, None, :] * same).reshape(64, 32)


def latent_out(mix, tile, **kw):
    flat = call(
        latent_kernel, "latent", (mix, tile, SPREAD), [((512, NZ), F32)],
        [pltpu.VMEM((32, 8 * NZ), F32)], **kw,
    )[0]
    return flat.reshape(8, 32, 2, NZ).transpose(0, 2, 1, 3).reshape(8, 2, 4096)


def swaps(lower):
    return [pair for i in lower for pair in ((i, i + 1), (i + 1, i))]


def body(wave_now, wave_prev, courant, forward, receivers, residual, aperture, latent, weight):
    cur, prev = wave_now[0], wave_prev[0]
    rec, res = receivers.transpose(1, 0, 2), residual.transpose(1, 0, 2)
    outer, inner, begun = head(cur, prev, courant, rec, res)
    count = lax.axis_size(SLAB)
    outer = lax.ppermute(outer, SLAB, swaps(range(1, count - 1, 2)))
    inner = lax.ppermute(inner, SLAB, swaps(range(0, count, 2)))
    second, third, fwd = inject(forward[0], rec, res)
    lat = latent_rows(latent)
    mix = mixing(weight)
    rows, after, before = wave(
        cur, courant, aperture, fwd, begun, second, third, outer, inner
    )
    near = gather_sum(lax.all_to_all(rows, "y", 0, 0, tiled=True))
    pieces = lax.all_to_all(near, "zh", 0, 0, tiled=True)
    after, before = store(after, before)
    pieces, after, before, lat, mix = lax.optimization_barrier((pieces, after, before, lat, mix))
    tile, shares = decode(pieces, lat)
    latent_grad = latent_out(mix, tile)
    shares = lax.all_to_all(shares, ("y", "x", "c"), 0, 0, tiled=True)
    shares, latent_grad = lax.optimization_barrier((shares, latent_grad))
    shares = call(share_kernel, "share", (shares,), [((16, 4, 128), F32)])[0]
    shares = lax.all_to_all(shares, ("zh", "zl"), 0, 0, tiled=True)

    def last(pieces, out):
        final_kernel(pieces, out, scale=1.0 / math.sqrt(256 * 32 * 64))

    weight_grad = call(last, "total", (shares,), [((8, 64), F32)])[0].T
    return (after[None], before[None], latent_grad, weight_grad)


def solution(mesh):
    fine = Mesh(mesh.devices.reshape(4, 4, 4, 4, 2), PARTS)
    return jax.shard_map(
        body,
        mesh=fine,
        in_specs=(
            P(SHOT, SLAB, None, None),
            P(SHOT, SLAB, None, None),
            P(SLAB, None, None),
            P(SHOT, None, SLAB, None, None),
            P(SHOT, None, None),
            P(SHOT, None, None),
            P(SHOT, None),
            P(SLAB, SHOT, None),
            P(),
        ),
        out_specs=(
            P(SHOT, SLAB, None, None),
            P(SHOT, SLAB, None, None),
            P(SLAB, SHOT, None),
            P(),
        ),
        check_vma=False,
    )
```
